128 devices in a mesh: seq: 32 (over x, y_lo, z), head: 4 (over y_hi, core).
Axes of the slice: x: 4, y: 4 (y_hi: 2, y_lo: 2; y = y_hi * 2 + y_lo), z: 4, core: 2. Of those that a mesh axis runs over, the one named last changes fastest.
Arguments:
- queries: bfloat16 [16384, 1536], P('seq', 'head'), may hold values from -6 to 6
- keys: bfloat16 [16384, 1536], P('seq', 'head'), may hold values from -6 to 6
- values: bfloat16 [16384, 1536], P('seq', 'head'), may hold values from -6 to 6
- upstream_out: bfloat16 [16384, 1536], P('seq'), may hold values from -192 to 192
- out_weight: bfloat16 [1536, 1536], P('head'), may hold values from -0.15625 to 0.15625
- qkv_weight: bfloat16 [3, 1536, 1536], P(None, None, 'head'), may hold values from -0.15625 to 0.15625
- rand_links: int32 [128, 3], replicated, may hold values from 0 to 127, as said below
- global_links: int32 [2], replicated, may hold values from 0 to 127, as said below
Outputs:
- grad_input: bfloat16 [1536, 16384], P('head', 'seq')
The draws below stay inside these ranges and needn't reach their ends.
Inputs may be any that keep to these rules, and one draw needn't show every extreme that they name: `rand_links`: counting each of the 2 global blocks once, the 14 blocks named by a run of 4 consecutive query blocks starting at a multiple of 4 fall at most 2 times into any run of 4 consecutive key blocks starting at a multiple of 4, and exactly 2 times into some such run. `global_links`: the 2 blocks differ; the last block of the sequence is always one of them.
All inputs are finite; a program needn't handle non-finite values.
Results may differ from the reference program's by a relative error of at most 0.02.
Values may be sent and summed in bfloat16 or wider, within the bound.
No kernel may reach another device: no remote copies, remote signals or barrier semaphores. Data moves between devices by JAX's collectives and lax.ppermute only.
A program may use at most 192 MiB of HBM per device.

```python
import jax
import jax.numpy as jnp
from jax import lax

D = 1536
HEADS = 12
HD = 128
BLK = 128
R = 3
G = 2
BLK_DEV = 4
NBLK = 128
TOKENS = 16384
HF = 1536
NKEY = 8
CAP = 2


def drawn_rows(key):
    first = jax.random.fold_in(key, 0)
    return jax.random.truncated_normal(first, -6.0, 6.0, (TOKENS, HF), jnp.float32)


def draw_queries(key, part):
    vals = drawn_rows(jax.random.fold_in(key, 11))
    return vals.astype(jnp.bfloat16)


def draw_keys(key, part):
    vals = drawn_rows(jax.random.fold_in(key, 13))
    return vals.astype(jnp.bfloat16)


def global_blocks(key):
    others = jax.random.permutation(jax.random.fold_in(key, 101), NBLK - 1)[:G - 1].astype(jnp.int32)
    chosen = jnp.concatenate([jnp.full((1,), NBLK - 1, jnp.int32), others])
    order = jax.random.permutation(jax.random.fold_in(key, 102), G)
    return chosen[order].astype(jnp.int32)


def draw_global_links(key, part):
    return global_blocks(key)


def draw_rand_links(key, part):
    groups = NBLK // BLK_DEV
    links = BLK_DEV * R
    glob_owner = global_blocks(key) // BLK_DEV
    glob_count = jnp.sum((glob_owner[:, None] == jnp.arange(groups, dtype=jnp.int32)[None, :]).astype(jnp.int32), axis=0)
    owners = jnp.repeat(jnp.arange(groups, dtype=jnp.int32), CAP)
    copies = jnp.tile(jnp.arange(CAP, dtype=jnp.int32), groups)
    usable = copies >= glob_count[owners]

    def one_group(sub):
        first, second, third, fourth = jax.random.split(sub, 4)
        special = jax.random.randint(first, (), 0, groups)
        scores = jax.random.permutation(second, groups * CAP).astype(jnp.int32)
        scores = jnp.where(owners == special, -1, scores)
        scores = jnp.where(usable, scores, groups * CAP + 1)
        order = jnp.argsort(scores, stable=True)
        chosen = owners[order[:links]]
        chosen = chosen[jax.random.permutation(third, links)]
        local = jax.random.randint(fourth, (links,), 0, BLK_DEV)
        return (chosen * BLK_DEV + local).astype(jnp.int32)
    subkeys = jax.random.split(jax.random.fold_in(key, 202), groups)
    return jax.vmap(one_group)(subkeys).reshape(NBLK, R).astype(jnp.int32)


def shard_levels(rng, shape, shards, least, top_value):
    loudness, own = 1.0, jax.random.fold_in(rng, 6)
    for dim, parts in shards:
        draws = jnp.exp(jax.random.uniform(jax.random.fold_in(own, dim), (parts,), jnp.float32, least / len(shards), top_value / len(shards)))
        loudness = loudness * jnp.repeat(draws, shape[dim] // parts).reshape([-1 if axis == dim else 1 for axis in range(len(shape))])
    return loudness


def gaussian(key, extent, deviation, reach, shards=(), kind=jnp.bfloat16):
    result = deviation * jax.random.normal(key, extent, jnp.float32)
    if shards:
        result = result * shard_levels(key, extent, shards, -0.22, 0.18)
    return jnp.clip(result, -reach, reach).astype(kind)


def setup_inputs(seed: int = 0) -> dict:
    arg_keys = jax.random.split(jax.random.key(seed), 9)
    return {
        "queries": draw_queries(jax.random.fold_in(arg_keys[8], 71), 0),
        "keys": draw_keys(jax.random.fold_in(arg_keys[8], 71), 0),
        "values": gaussian(arg_keys[2], (TOKENS, HF), 1.0, 6.0, ((0, 32), (1, 4))),
        "upstream_out": gaussian(arg_keys[3], (TOKENS, D), 32.0, 192.0, ((0, 32),)),
        "out_weight": gaussian(arg_keys[4], (HF, D), HF ** -0.5, 0.15625, ((0, 4),)),
        "qkv_weight": gaussian(arg_keys[5], (3, D, HF), D ** -0.5, 0.15625, ((2, 4),)),
        "rand_links": draw_rand_links(jax.random.fold_in(arg_keys[8], 71), 0),
        "global_links": draw_global_links(jax.random.fold_in(arg_keys[8], 71), 0),
    }


def group_grads(queries, upstream, keys, values, scale):
    f32 = jnp.float32
    scores = jnp.einsum("bqhd,bkhd->bhqk", queries.astype(f32), keys.astype(f32)) * scale
    peak = jnp.max(scores, axis=-1, keepdims=True)
    log_total = peak + jnp.log(jnp.sum(jnp.exp(scores - peak), axis=-1, keepdims=True))
    probs = jnp.exp(scores - log_total)
    slope = jnp.einsum("bqhd,bkhd->bhqk", upstream.astype(f32), values.astype(f32))
    weighted = jnp.sum(probs * slope, axis=-1, keepdims=True)
    coeff = (probs * (slope - weighted)).astype(jnp.bfloat16).astype(f32)
    probs_low = probs.astype(jnp.bfloat16).astype(f32)
    query_part = jnp.einsum("bhqk,bkhd->bqhd", coeff, keys.astype(f32)) * scale
    key_part = jnp.einsum("bhqk,bqhd->bkhd", coeff, queries.astype(f32)) * scale
    value_part = jnp.einsum("bhqk,bqhd->bkhd", probs_low, upstream.astype(f32))
    return query_part, key_part, value_part


def rounded(array):
    return lax.optimization_barrier(array.astype(jnp.bfloat16)).astype(jnp.float32)


def reference(queries, keys, values, upstream_out, out_weight, qkv_weight, rand_links, global_links):
    scale = HD ** -0.5
    grad_context = jnp.dot(upstream_out, out_weight.T, preferred_element_type=jnp.float32).astype(jnp.bfloat16)
    query_blocks = queries.reshape(NBLK, BLK, HEADS, HD)
    context_blocks = grad_context.reshape(NBLK, BLK, HEADS, HD)
    key_blocks = keys.reshape(NBLK, BLK, HEADS, HD)
    value_blocks = values.reshape(NBLK, BLK, HEADS, HD)
    groups = NBLK // BLK_DEV

    def group_step(carry, index):
        key_acc, value_acc = carry
        blocks = index * BLK_DEV + jnp.arange(BLK_DEV, dtype=jnp.int32)
        window = (blocks[:, None] + jnp.arange(-1, 2, dtype=jnp.int32)[None, :]) % NBLK
        randoms = rand_links[blocks]
        globs = jnp.broadcast_to(global_links[None, :], (BLK_DEV, G))
        key_ids = jnp.concatenate([window, randoms, globs], axis=1)
        gathered_keys = key_blocks[key_ids].reshape(BLK_DEV, NKEY * BLK, HEADS, HD)
        gathered_values = value_blocks[key_ids].reshape(BLK_DEV, NKEY * BLK, HEADS, HD)
        query_part, key_part, value_part = group_grads(query_blocks[blocks], context_blocks[blocks], gathered_keys, gathered_values, scale)
        key_part = key_part.reshape(BLK_DEV, NKEY, BLK, HF)
        value_part = value_part.reshape(BLK_DEV, NKEY, BLK, HF)
        key_acc = key_acc.at[window].add(key_part[:, :3])
        value_acc = value_acc.at[window].add(value_part[:, :3])
        key_acc = key_acc.at[randoms].add(rounded(key_part[:, 3:3 + R]))
        value_acc = value_acc.at[randoms].add(rounded(value_part[:, 3:3 + R]))
        key_acc = key_acc.at[global_links].add(rounded(jnp.sum(key_part[:, 3 + R:], axis=0)))
        value_acc = value_acc.at[global_links].add(rounded(jnp.sum(value_part[:, 3 + R:], axis=0)))
        grad_q = query_part.reshape(BLK_DEV * BLK, HF).astype(jnp.bfloat16)
        return (key_acc, value_acc), grad_q

    start = (jnp.zeros((NBLK, BLK, HF), jnp.float32), jnp.zeros((NBLK, BLK, HF), jnp.float32))
    (key_acc, value_acc), grad_q = lax.scan(group_step, start, jnp.arange(groups, dtype=jnp.int32))
    grad_queries = grad_q.reshape(TOKENS, HF)
    grad_keys = key_acc.reshape(TOKENS, HF).astype(jnp.bfloat16)
    grad_values = value_acc.reshape(TOKENS, HF).astype(jnp.bfloat16)
    total = jnp.dot(qkv_weight[0], grad_queries.T, preferred_element_type=jnp.float32)
    total = total + jnp.dot(qkv_weight[1], grad_keys.T, preferred_element_type=jnp.float32)
    total = total + jnp.dot(qkv_weight[2], grad_values.T, preferred_element_type=jnp.float32)
    return total.astype(jnp.bfloat16)
```

```python
import functools

import jax
import jax.numpy as jnp
from jax import lax
from jax.experimental import pallas as pl
from jax.experimental.pallas import tpu as pltpu
from jax.sharding import PartitionSpec as P

HD = 128
BLK = 128
R = 3
G = 2
BLK_DEV = 4
NKEY = 3 + R + G
AXES = ("seq", "head")
LINE = 4
NQ = LINE * BLK_DEV
ROWS = NQ * BLK
NSHARD = 8
HALF = ROWS // 2
F32 = jnp.float32
BF16 = jnp.bfloat16


def moved(dev, ring, pair, line):
    h, s = dev % 4, dev // 4
    x, y, z = s // 8, (s // 4) % 2, s % 4
    if h % 2 == 0:
        x, z = (x + ring) % 4, (z + line) % 4
    else:
        z, x = (z + ring) % 4, (x + line) % 4
    y = (y + pair) % 2
    return ((x * 2 + y) * 4 + z) * 4 + h


def line_pos(dev):
    h, s = dev % 4, dev // 4
    return s % 4 if h % 2 == 0 else s // 8


DEVS = range(128)
DEAL = {
    k: [(d, moved(d, 0, 0, k)) for d in DEVS if line_pos(moved(d, 0, 0, k)) < 3] for k in (1, 2, 3)
}
BACK = {k: [(t, d) for d, t in DEAL[k]] for k in (1, 2, 3)}
RING = {k: [(d, moved(d, k, 0, 0)) for d in DEVS if line_pos(d) < 3] for k in (1, -1)}
PAIR = [(d, moved(d, 0, 1, 0)) for d in DEVS if line_pos(d) < 3]
CORE = [(d, d ^ 1) for d in DEVS]
FAR = [(d, d ^ 2) for d in DEVS]


def send(x, perm):
    return lax.ppermute(x, AXES, perm)


def attend_kernel(table, qd_ref, *refs):
    kv_refs = refs[:NSHARD]
    gq_ref = refs[NSHARD]
    out_refs = refs[NSHARD + 1 : 2 * NSHARD + 1]
    kv, acc, kv_now, sems = refs[2 * NSHARD + 1 :]
    scale = HD ** (-0.5)
    copies = [
        pltpu.make_async_copy(kv_refs[n], kv.at[pl.ds(n * ROWS, ROWS)], sems.at[n])
        for n in range(NSHARD)
    ]
    for c in copies:
        c.start()

    def zero(n, carry):
        acc[pl.ds(n * BLK, BLK), :] = jnp.zeros((BLK, 2 * HD), F32)
        return carry

    lax.fori_loop(0, NSHARD * NQ, zero, 0)
    for c in copies:
        c.wait()

    def step(n, carry):
        rows = pl.ds(pl.multiple_of(n * BLK, BLK), BLK)
        q = qd_ref[rows, :HD]
        d = qd_ref[rows, HD:]
        for j in range(NKEY):
            at = pl.multiple_of(table[n, j] * BLK, BLK)
            kv_now[j * BLK : (j + 1) * BLK, :] = kv[pl.ds(at, BLK), :]
        k = kv_now[:, :HD]
        v = kv_now[:, HD:]
        nt = (((1,), (1,)), ((), ()))
        scores = lax.dot_general(k, q, nt, preferred_element_type=F32)
        slope = lax.dot_general(v, d, nt, preferred_element_type=F32)
        peak = jnp.max(scores, axis=0, keepdims=True)
        e = jnp.exp((scores - peak) * scale)
        inv = 1.0 / jnp.sum(e, axis=0, keepdims=True)
        weighted = jnp.sum(e * slope, axis=0, keepdims=True) * inv
        probs = e * inv
        coeff = (probs * (slope - weighted)).astype(BF16)
        low = probs.astype(BF16)
        gq = lax.dot_general(coeff, k, (((0,), (0,)), ((), ())), preferred_element_type=F32)
        gq_ref[rows, :] = (gq * scale).astype(BF16)
        nn = (((1,), (0,)), ((), ()))
        gk = lax.dot_general(coeff, q, nn, preferred_element_type=F32)
        gv = lax.dot_general(low, d, nn, preferred_element_type=F32)
        for j in range(NKEY):
            at = pl.multiple_of(table[n, j] * BLK, BLK)
            part = slice(j * BLK, (j + 1) * BLK)
            acc[pl.ds(at, BLK), :HD] += gk[part]
            acc[pl.ds(at, BLK), HD:] += gv[part]
        return carry

    lax.fori_loop(0, NQ, step, 0)

    for m in range(NSHARD):

        def put(n, carry, m=m):
            rows = pl.ds(pl.multiple_of(n * BLK, BLK), BLK)
            src = pl.ds(pl.multiple_of(m * ROWS + n * BLK, BLK), BLK)
            out_refs[m][rows, :HD] = (acc[src, :HD] * scale).astype(BF16)
            out_refs[m][rows, HD:] = acc[src, HD:].astype(BF16)
            return carry

        lax.fori_loop(0, NQ, put, 0)


def attend(table, qd, shards):
    shard = jax.ShapeDtypeStruct((ROWS, 2 * HD), BF16)
    vmem = pl.BlockSpec(memory_space=pltpu.VMEM)
    out = pl.pallas_call(
        attend_kernel,
        name="attend",
        out_shape=(jax.ShapeDtypeStruct((ROWS, HD), BF16),) + (shard,) * NSHARD,
        grid_spec=pltpu.PrefetchScalarGridSpec(
            num_scalar_prefetch=1,
            grid=(),
            in_specs=[vmem] + [pl.BlockSpec(memory_space=pl.ANY)] * NSHARD,
            out_specs=(vmem,) * (NSHARD + 1),
            scratch_shapes=[
                pltpu.VMEM((NSHARD * ROWS, 2 * HD), BF16),
                pltpu.VMEM((NSHARD * ROWS, 2 * HD), F32),
                pltpu.VMEM((NKEY * BLK, 2 * HD), BF16),
                pltpu.SemaphoreType.DMA((NSHARD,)),
            ],
        ),
        compiler_params=pltpu.CompilerParams(vmem_limit_bytes=56 << 20),
    )(table, qd, *shards)
    return out[0], out[1:]


def add(*terms):
    return functools.reduce(lambda a, b: a + b, [t.astype(F32) for t in terms]).astype(BF16)


def ring_gather(shard):
    one = send(shard, RING[1])
    three = send(shard, RING[-1])
    two = jnp.concatenate([send(one[:HALF], RING[1]), send(three[HALF:], RING[-1])], axis=0)
    return [shard, one, two, three]


def ring_reduce(parts):
    zero, one, two, three = parts
    down = send(two[:HALF], RING[1])
    up = send(two[HALF:], RING[-1])
    three = jnp.concatenate([add(three[:HALF], down), three[HALF:]], axis=0)
    one = jnp.concatenate([one[:HALF], add(one[HALF:], up)], axis=0)
    return add(zero, send(three, RING[1]), send(one, RING[-1]))


def deal(pair, pos):
    heads = pair.reshape(2, BLK_DEV * BLK, 3, HD).transpose(2, 1, 0, 3)
    heads = heads.reshape(3, BLK_DEV * BLK, 2 * HD)

    def head(k):
        return lax.dynamic_index_in_dim(heads, jnp.minimum((pos + k) % 4, 2), 0, keepdims=False)

    return jnp.concatenate([head(0)] + [send(head(k), DEAL[k]) for k in (1, 2, 3)], axis=0)


def give_back(grads, pos, width):
    grads = grads.reshape(LINE, BLK_DEV * BLK, width)
    got = jnp.stack([grads[0]] + [send(grads[k], BACK[k]) for k in (1, 2, 3)], axis=0)
    return jnp.stack(
        [lax.dynamic_index_in_dim(got, (p - pos) % 4, 0, keepdims=False) for p in range(3)], axis=0
    )


def body(queries, keys, values, upstream_out, out_weight, qkv_weight, rand_links, global_links):
    s = lax.axis_index("seq")
    h = lax.axis_index("head")
    x, y, z = s // 8, (s // 4) % 2, s % 4
    core = h % 2
    ring = jnp.where(core == 0, x, z)
    pos = jnp.where(core == 0, z, x)

    n = jnp.arange(NQ, dtype=jnp.int32)
    line = (pos - n // BLK_DEV) % 4
    seq = jnp.where(core == 0, (x * 2 + y) * 4 + line, (line * 2 + y) * 4 + z)
    block = seq * BLK_DEV + n % BLK_DEV
    total = rand_links.shape[0]
    mine = block[:, None, None] == jnp.arange(total, dtype=jnp.int32)[None, :, None]
    rand = jnp.sum(jnp.where(mine, rand_links[None], 0), axis=1)
    window = (block[:, None] + jnp.arange(-1, 2, dtype=jnp.int32)[None]) % total
    glob = jnp.broadcast_to(global_links[None], (NQ, G))
    key = jnp.concatenate([window, rand, glob], axis=1)
    ks = key // BLK_DEV
    kx, ky, kz = ks // 8, (ks // 4) % 2, ks % 4
    k_ring = jnp.where(core == 0, kx, kz)
    k_pos = jnp.where(core == 0, kz, kx)
    shard_of = jnp.where(ky == y, 0, 4) + (ring - k_ring) % 4
    table = shard_of * NQ + ((pos - k_pos) % 4) * BLK_DEV + key % BLK_DEV

    own = deal(jnp.stack([keys, values], axis=0), pos)
    other = send(own, PAIR)
    shards = ring_gather(own) + ring_gather(other)
    grad_ctx = lax.dot_general(
        upstream_out, out_weight, (((1,), (1,)), ((), ())), preferred_element_type=F32
    ).astype(BF16)
    qd = deal(jnp.stack([queries, grad_ctx], axis=0), pos)
    grad_q, parts = attend(table, qd, shards)

    other_sum = ring_reduce(parts[4:])
    own_sum = ring_reduce(parts[:4])
    grad_kv = add(own_sum, send(other_sum, PAIR))
    q_back = give_back(grad_q, pos, HD)
    kv_back = give_back(grad_kv, pos, 2 * HD)
    stacked = jnp.stack([q_back, kv_back[:, :, :HD], kv_back[:, :, HD:]], axis=0)
    weight = qkv_weight.reshape(3, qkv_weight.shape[1], 3, HD)
    share = lax.dot_general(
        weight, stacked, (((0, 2, 3), (0, 1, 3)), ((), ())), preferred_element_type=F32
    ).astype(BF16)
    share = share.reshape(2, 2, share.shape[0] // 4, share.shape[1])
    mine_of = lax.dynamic_index_in_dim(share, core, 1, keepdims=False)
    theirs = lax.dynamic_index_in_dim(share, 1 - core, 1, keepdims=False)
    both = add(mine_of, send(theirs, CORE))
    far = h // 2
    keep = lax.dynamic_index_in_dim(both, far, 0, keepdims=False)
    give = lax.dynamic_index_in_dim(both, 1 - far, 0, keepdims=False)
    return add(keep, send(give, FAR))


def solution(mesh):
    in_specs = (
        P("seq", "head"),
        P("seq", "head"),
        P("seq", "head"),
        P("seq", None),
        P("head", None),
        P(None, None, "head"),
        P(),
        P(),
    )
    out_specs = P("head", "seq")
    return jax.shard_map(body, mesh=mesh, in_specs=in_specs, out_specs=out_specs, check_vma=False)
```

```python
import functools

import jax
import jax.numpy as jnp
from jax import lax
from jax.experimental import pallas as pl
from jax.experimental.pallas import tpu as pltpu
from jax.sharding import PartitionSpec as P

HD = 128
BLK = 128
R = 3
G = 2
BLK_DEV = 4
NKEY = 3 + R + G
AXES = ("seq", "head")
LINE = 4
NQ = LINE * BLK_DEV
ROWS = NQ * BLK
NSHARD = 8
F32 = jnp.float32
BF16 = jnp.bfloat16


def moved(dev, ring, pair, line):
    h, s = dev % 4, dev // 4
    x, y, z = s // 8, (s // 4) % 2, s % 4
    if h % 2 == 0:
        x, z = (x + ring) % 4, (z + line) % 4
    else:
        z, x = (z + ring) % 4, (x + line) % 4
    y = (y + pair) % 2
    return ((x * 2 + y) * 4 + z) * 4 + h


def line_pos(dev):
    h, s = dev % 4, dev // 4
    return s % 4 if h % 2 == 0 else s // 8


DEVS = range(128)


def groups(step):
    seen, out = set(), []
    for d in DEVS:
        if d not in seen:
            out.append([d] + [step(d, k) for k in (1, 2, 3)])
            seen.update(out[-1])
    return out


LINES = groups(lambda d, k: moved(d, 0, 0, k))
RINGS = groups(lambda d, k: moved(d, k, 0, 0))
PAIR = [(d, moved(d, 0, 1, 0)) for d in DEVS if line_pos(d) < 3]
CORE = [(d, d ^ 1) for d in DEVS]
FAR = [(d, d ^ 2) for d in DEVS]


def send(x, perm):
    return lax.ppermute(x, AXES, perm)


def attend_kernel(table, qd_ref, own_ref, other_ref, gq_ref, own_out, other_out, kv, acc, kv_now, qd_now, sems):
    scale = HD ** (-0.5)
    side = NSHARD // 2 * ROWS
    copies = [
        pltpu.make_async_copy(ref, kv.at[pl.ds(n * side, side)], sems.at[n])
        for n, ref in enumerate((own_ref, other_ref))
    ]
    for c in copies:
        c.start()

    def zero(n, carry):
        acc[pl.ds(n * BLK, BLK), :] = jnp.zeros((BLK, 2 * HD), F32)
        return carry

    lax.fori_loop(0, NSHARD * NQ, zero, 0, unroll=4)
    qd_now[...] = jnp.zeros((2 * BLK, 2 * HD), BF16)
    for c in copies:
        c.wait()

    def step(n, carry):
        rows = pl.ds(pl.multiple_of(n * BLK, BLK), BLK)
        qd_now[:BLK, :HD] = qd_ref[rows, :HD]
        qd_now[BLK:, HD:] = qd_ref[rows, HD:]
        qd = qd_now[...]
        for j in range(NKEY):
            at = pl.multiple_of(table[n, j] * BLK, BLK)
            kv_now[j * BLK : (j + 1) * BLK, :] = kv[pl.ds(at, BLK), :]
        both = lax.dot_general(
            kv_now[...], qd, (((1,), (1,)), ((), ())), preferred_element_type=F32
        )
        scores, slope = both[:, :BLK], both[:, BLK:]
        peak = jnp.max(scores, axis=0, keepdims=True)
        e = jnp.exp((scores - peak) * scale)
        inv = 1.0 / jnp.sum(e, axis=0, keepdims=True)
        weighted = jnp.sum(e * slope, axis=0, keepdims=True) * inv
        probs = e * inv
        coeff = (probs * (slope - weighted)).astype(BF16)
        gq = lax.dot_general(
            coeff, kv_now[:, :HD], (((0,), (0,)), ((), ())), preferred_element_type=F32
        )
        gq_ref[rows, :] = (gq * scale).astype(BF16)
        gkv = lax.dot_general(
            jnp.concatenate([coeff, probs.astype(BF16)], axis=1),
            qd,
            (((1,), (0,)), ((), ())),
            preferred_element_type=F32,
        )
        for j in range(NKEY):
            at = pl.multiple_of(table[n, j] * BLK, BLK)
            acc[pl.ds(at, BLK), :] += gkv[j * BLK : (j + 1) * BLK]
        return carry

    lax.fori_loop(0, NQ, step, 0)

    for m, out in enumerate((own_out, other_out)):

        def put(n, carry, m=m, out=out):
            rows = pl.ds(pl.multiple_of(n * BLK, BLK), BLK)
            src = pl.ds(pl.multiple_of(m * side + n * BLK, BLK), BLK)
            out[rows, :HD] = (acc[src, :HD] * scale).astype(BF16)
            out[rows, HD:] = acc[src, HD:].astype(BF16)
            return carry

        lax.fori_loop(0, side // BLK, put, 0, unroll=2)


def attend(table, qd, own_row, other_row):
    side = jax.ShapeDtypeStruct(own_row.shape, BF16)
    vmem = pl.BlockSpec(memory_space=pltpu.VMEM)
    return pl.pallas_call(
        attend_kernel,
        name="attend",
        out_shape=(jax.ShapeDtypeStruct((ROWS, HD), BF16), side, side),
        grid_spec=pltpu.PrefetchScalarGridSpec(
            num_scalar_prefetch=1,
            grid=(),
            in_specs=[vmem] + [pl.BlockSpec(memory_space=pl.ANY)] * 2,
            out_specs=(vmem,) * 3,
            scratch_shapes=[
                pltpu.VMEM((NSHARD * ROWS, 2 * HD), BF16),
                pltpu.VMEM((NSHARD * ROWS, 2 * HD), F32),
                pltpu.VMEM((NKEY * BLK, 2 * HD), BF16),
                pltpu.VMEM((2 * BLK, 2 * HD), BF16),
                pltpu.SemaphoreType.DMA((2,)),
            ],
        ),
        compiler_params=pltpu.CompilerParams(vmem_limit_bytes=56 << 20),
    )(table, qd, own_row, other_row)


def add(*terms):
    return functools.reduce(lambda a, b: a + b, [t.astype(F32) for t in terms]).astype(BF16)


def exchange(x, who):
    return lax.all_to_all(x, AXES, 0, 0, axis_index_groups=who, tiled=True)


def ring_gather(shard):
    return exchange(jnp.concatenate([shard] * 4, axis=0), RINGS)


def ring_reduce(parts):
    return exchange(parts, RINGS).reshape(4, ROWS, -1)


def deal(pair):
    heads = pair.reshape(2, BLK_DEV * BLK, 3, HD).transpose(2, 1, 0, 3)
    heads = heads.reshape(3, BLK_DEV * BLK, 2 * HD)
    return exchange(jnp.concatenate([heads, heads[:1]], axis=0), LINES).reshape(ROWS, 2 * HD)


def give_back(grads, width):
    return exchange(grads.reshape(LINE, BLK_DEV * BLK, width), LINES)[:3]


def body(queries, keys, values, upstream_out, out_weight, qkv_weight, rand_links, global_links):
    s = lax.axis_index("seq")
    h = lax.axis_index("head")
    x, y, z = s // 8, (s // 4) % 2, s % 4
    core = h % 2

    n = jnp.arange(NQ, dtype=jnp.int32)
    line = n // BLK_DEV
    seq = jnp.where(core == 0, (x * 2 + y) * 4 + line, (line * 2 + y) * 4 + z)
    block = seq * BLK_DEV + n % BLK_DEV
    total = rand_links.shape[0]
    mine = block[:, None, None] == jnp.arange(total, dtype=jnp.int32)[None, :, None]
    rand = jnp.sum(jnp.where(mine, rand_links[None], 0), axis=1)
    window = (block[:, None] + jnp.arange(-1, 2, dtype=jnp.int32)[None]) % total
    glob = jnp.broadcast_to(global_links[None], (NQ, G))
    key = jnp.concatenate([window, rand, glob], axis=1)
    ks = key // BLK_DEV
    kx, ky, kz = ks // 8, (ks // 4) % 2, ks % 4
    k_ring = jnp.where(core == 0, kx, kz)
    k_pos = jnp.where(core == 0, kz, kx)
    shard_of = jnp.where(ky == y, 0, 4) + k_ring
    table = (shard_of * LINE + k_pos) * BLK_DEV + key % BLK_DEV

    own = deal(jnp.stack([keys, values], axis=0))
    other = send(own, PAIR)
    own_row = ring_gather(own)
    grad_ctx = lax.dot_general(
        upstream_out, out_weight, (((1,), (1,)), ((), ())), preferred_element_type=F32
    ).astype(BF16)
    qd = deal(jnp.stack([queries, grad_ctx], axis=0))
    grad_q, own_parts, other_parts = attend(table, qd, own_row, ring_gather(other))

    other_sum = add(*ring_reduce(other_parts))
    grad_kv = add(*ring_reduce(own_parts), send(other_sum, PAIR))
    q_back = give_back(grad_q, HD)
    kv_back = give_back(grad_kv, 2 * HD)
    stacked = jnp.stack([q_back, kv_back[:, :, :HD], kv_back[:, :, HD:]], axis=0)
    weight = qkv_weight.reshape(3, qkv_weight.shape[1], 3, HD)
    share = lax.dot_general(
        weight, stacked, (((0, 2, 3), (0, 1, 3)), ((), ())), preferred_element_type=F32
    ).astype(BF16)
    share = share.reshape(2, 2, share.shape[0] // 4, share.shape[1])
    mine_of = lax.dynamic_index_in_dim(share, core, 1, keepdims=False)
    theirs = lax.dynamic_index_in_dim(share, 1 - core, 1, keepdims=False)
    both = add(mine_of, send(theirs, CORE))
    far = h // 2
    keep = lax.dynamic_index_in_dim(both, far, 0, keepdims=False)
    give = lax.dynamic_index_in_dim(both, 1 - far, 0, keepdims=False)
    return add(keep, send(give, FAR))


def solution(mesh):
    in_specs = (
        P("seq", "head"),
        P("seq", "head"),
        P("seq", "head"),
        P("seq", None),
        P("head", None),
        P(None, None, "head"),
        P(),
        P(),
    )
    out_specs = P("head", "seq")
    return jax.shard_map(body, mesh=mesh, in_specs=in_specs, out_specs=out_specs, check_vma=False)
```

```python
import functools

import jax
import jax.numpy as jnp
from jax import lax
from jax.experimental import pallas as pl
from jax.experimental.pallas import tpu as pltpu
from jax.sharding import PartitionSpec as P

HD = 128
BLK = 128
R = 3
G = 2
BLK_DEV = 4
NKEY = 3 + R + G
AXES = ("seq", "head")
LINE = 4
NQ = LINE * BLK_DEV
ROWS = NQ * BLK
NSHARD = 8
F32 = jnp.float32
BF16 = jnp.bfloat16


def moved(dev, ring, pair, line):
    h, s = dev % 4, dev // 4
    x, y, z = s // 8, (s // 4) % 2, s % 4
    if h % 2 == 0:
        x, z = (x + ring) % 4, (z + line) % 4
    else:
        z, x = (z + ring) % 4, (x + line) % 4
    y = (y + pair) % 2
    return ((x * 2 + y) * 4 + z) * 4 + h


def line_pos(dev):
    h, s = dev % 4, dev // 4
    return s % 4 if h % 2 == 0 else s // 8


DEVS = range(128)


def groups(step):
    seen, out = set(), []
    for d in DEVS:
        if d not in seen:
            out.append([d] + [step(d, k) for k in (1, 2, 3)])
            seen.update(out[-1])
    return out


LINES = groups(lambda d, k: moved(d, 0, 0, k))
RING = {k: [(d, moved(d, k, 0, 0)) for d in DEVS if line_pos(d) < 3] for k in (1, 2, 3)}
PAIR = [(d, moved(d, 0, 1, 0)) for d in DEVS if line_pos(d) < 3]
CORE = [(d, d ^ 1) for d in DEVS]
FAR = [(d, d ^ 2) for d in DEVS]


def send(x, perm):
    return lax.ppermute(x, AXES, perm)


def attend_kernel(table, qd_ref, *refs):
    kv_refs, gq_ref = refs[:NSHARD], refs[NSHARD]
    out_refs = refs[NSHARD + 1 : 2 * NSHARD + 1]
    kv, acc, kv_now, stage, in_sems, out_sems = refs[2 * NSHARD + 1 :]
    scale = HD ** (-0.5)
    loads = [
        pltpu.make_async_copy(kv_refs[m], kv.at[pl.ds(m * ROWS, ROWS)], in_sems.at[m])
        for m in range(NSHARD)
    ]
    for c in loads:
        c.start()

    def zero(n, carry):
        acc[pl.ds(pl.multiple_of(n * BLK, BLK), BLK), :] = jnp.zeros((BLK, 2 * HD), F32)
        return carry

    lax.fori_loop(0, NSHARD * NQ, zero, 0, unroll=2)
    for c in loads:
        c.wait()

    nt = (((1,), (1,)), ((), ()))
    nn = (((1,), (0,)), ((), ()))
    tn = (((0,), (0,)), ((), ()))

    def step(n, carry):
        rows = pl.ds(pl.multiple_of(n * BLK, BLK), BLK)
        q = qd_ref[rows, :HD]
        d = qd_ref[rows, HD:]
        at = [pl.multiple_of(table[n, j] * BLK, BLK) for j in range(NKEY)]
        for j in range(NKEY):
            kv_now[j * BLK : (j + 1) * BLK, :] = kv[pl.ds(at[j], BLK), :]
        scores = lax.dot_general(kv_now[:, :HD], q, nt, preferred_element_type=F32)
        slope = lax.dot_general(kv_now[:, HD:], d, nt, preferred_element_type=F32)
        peak = jnp.max(scores, axis=0, keepdims=True)
        e = jnp.exp((scores - peak) * scale)
        inv = 1.0 / jnp.sum(e, axis=0, keepdims=True)
        weighted = jnp.sum(e * slope, axis=0, keepdims=True) * inv
        probs = e * inv
        coeff = (probs * (slope - weighted)).astype(BF16)
        low = probs.astype(BF16)
        gq = lax.dot_general(coeff, kv_now[:, :HD], tn, preferred_element_type=F32)
        gq_ref[rows, :] = (gq * scale).astype(BF16)
        gk = lax.dot_general(coeff, q, nn, preferred_element_type=F32)
        gv = lax.dot_general(low, d, nn, preferred_element_type=F32)
        for j in range(NKEY):
            part = slice(j * BLK, (j + 1) * BLK)
            acc[pl.ds(at[j], BLK), :HD] += gk[part]
            acc[pl.ds(at[j], BLK), HD:] += gv[part]
        return carry

    lax.fori_loop(0, NQ, step, 0, unroll=2)

    stores = [pltpu.make_async_copy(stage.at[m], out_refs[m], out_sems.at[m]) for m in range(NSHARD)]
    for m in range(NSHARD):

        def put(n, carry, m=m):
            rows = pl.ds(pl.multiple_of(n * BLK, BLK), BLK)
            src = pl.ds(pl.multiple_of(m * ROWS + n * BLK, BLK), BLK)
            stage[m, rows, :HD] = (acc[src, :HD] * scale).astype(BF16)
            stage[m, rows, HD:] = acc[src, HD:].astype(BF16)
            return carry

        lax.fori_loop(0, NQ, put, 0, unroll=2)
        stores[m].start()
    for c in stores:
        c.wait()


def attend(table, qd, shards):
    shard = jax.ShapeDtypeStruct((ROWS, 2 * HD), BF16)
    vmem = pl.BlockSpec(memory_space=pltpu.VMEM)
    far = pl.BlockSpec(memory_space=pl.ANY)
    out = pl.pallas_call(
        attend_kernel,
        name="attend",
        out_shape=(jax.ShapeDtypeStruct((ROWS, HD), BF16),) + (shard,) * NSHARD,
        grid_spec=pltpu.PrefetchScalarGridSpec(
            num_scalar_prefetch=1,
            grid=(),
            in_specs=[vmem] + [far] * NSHARD,
            out_specs=(vmem,) + (far,) * NSHARD,
            scratch_shapes=[
                pltpu.VMEM((NSHARD * ROWS, 2 * HD), BF16),
                pltpu.VMEM((NSHARD * ROWS, 2 * HD), F32),
                pltpu.VMEM((NKEY * BLK, 2 * HD), BF16),
                pltpu.VMEM((NSHARD, ROWS, 2 * HD), BF16),
                pltpu.SemaphoreType.DMA((NSHARD,)),
                pltpu.SemaphoreType.DMA((NSHARD,)),
            ],
        ),
        compiler_params=pltpu.CompilerParams(vmem_limit_bytes=56 << 20),
    )(table, qd, *shards)
    return out[0], out[1:]


def add(*terms):
    return functools.reduce(lambda a, b: a + b, [t.astype(F32) for t in terms]).astype(BF16)


def exchange(x):
    return lax.all_to_all(x, AXES, 0, 0, axis_index_groups=LINES, tiled=True)


def deal(a, b):
    heads = [
        jnp.concatenate([a[:, p * HD : (p + 1) * HD], b[:, p * HD : (p + 1) * HD]], axis=1)
        for p in (0, 1, 2, 0)
    ]
    return exchange(jnp.concatenate(heads, axis=0))


def ring_gather(shard):
    return [shard] + [send(shard, RING[k]) for k in (3, 2, 1)]


def ring_sends(parts):
    return [parts[0]] + [send(parts[k], RING[k]) for k in (1, 3, 2)]


def body(queries, keys, values, upstream_out, out_weight, qkv_weight, rand_links, global_links):
    s = lax.axis_index("seq")
    h = lax.axis_index("head")
    x, y, z = s // 8, (s // 4) % 2, s % 4
    core, far = h % 2, h // 2
    ring = jnp.where(core == 0, x, z)

    n = jnp.arange(NQ, dtype=jnp.int32)
    line = n // BLK_DEV
    seq = jnp.where(core == 0, (x * 2 + y) * 4 + line, (line * 2 + y) * 4 + z)
    block = seq * BLK_DEV + n % BLK_DEV
    total = rand_links.shape[0]
    mine = block[:, None, None] == jnp.arange(total, dtype=jnp.int32)[None, :, None]
    rand = jnp.sum(jnp.where(mine, rand_links[None], 0), axis=1)
    window = (block[:, None] + jnp.arange(-1, 2, dtype=jnp.int32)[None]) % total
    glob = jnp.broadcast_to(global_links[None], (NQ, G))
    key = jnp.concatenate([window, rand, glob], axis=1)
    ks = key // BLK_DEV
    kx, ky, kz = ks // 8, (ks // 4) % 2, ks % 4
    k_ring = jnp.where(core == 0, kx, kz)
    k_pos = jnp.where(core == 0, kz, kx)
    shard_of = jnp.where(ky == y, 0, 4) + (k_ring - ring) % 4
    table = (shard_of * LINE + k_pos) * BLK_DEV + key % BLK_DEV

    own = deal(keys, values)
    other = send(own, PAIR)
    own_row = ring_gather(own)
    grad_ctx = lax.dot_general(
        upstream_out, out_weight, (((1,), (1,)), ((), ())), preferred_element_type=F32
    ).astype(BF16)
    grad_ctx, other = lax.optimization_barrier((grad_ctx, other))
    qd = deal(queries, grad_ctx)
    grad_q, parts = attend(table, qd, own_row + ring_gather(other))

    other_sum = add(*ring_sends(parts[4:]))
    own_sum = ring_sends(parts[:4])
    q_back = exchange(grad_q)
    other_sum, q_back = lax.optimization_barrier((other_sum, q_back))
    kv_back = exchange(add(*own_sum, send(other_sum, PAIR)))

    def tokens(back, lanes):
        back = back.reshape(LINE, BLK_DEV * BLK, -1)
        return jnp.concatenate([back[p, :, lanes] for p in range(3)], axis=1)

    grads = jnp.stack(
        [
            tokens(q_back, slice(0, HD)),
            tokens(kv_back, slice(0, HD)),
            tokens(kv_back, slice(HD, 2 * HD)),
        ],
        axis=0,
    )
    weight = qkv_weight.reshape(3, 2, 2, qkv_weight.shape[1] // 4, qkv_weight.shape[2])

    def share(to_far, to_core):
        w = lax.dynamic_index_in_dim(weight, to_far, 1, keepdims=False)
        w = lax.dynamic_index_in_dim(w, to_core, 1, keepdims=False)
        return lax.dot_general(
            w, grads, (((0, 2), (0, 2)), ((), ())), preferred_element_type=F32
        ).astype(BF16)

    from_far = send(add(share(1 - far, core), send(share(1 - far, 1 - core), CORE)), FAR)
    here = send(share(far, 1 - core), CORE)
    return add(share(far, core), here, from_far)


def solution(mesh):
    in_specs = (
        P("seq", "head"),
        P("seq", "head"),
        P("seq", "head"),
        P("seq", None),
        P("head", None),
        P(None, None, "head"),
        P(),
        P(),
    )
    out_specs = P("head", "seq")
    return jax.shard_map(body, mesh=mesh, in_specs=in_specs, out_specs=out_specs, check_vma=False)
```

```python
import functools

import jax
import jax.numpy as jnp
from jax import lax
from jax.experimental import pallas as pl
from jax.experimental.pallas import tpu as pltpu
from jax.sharding import PartitionSpec as P

HD = 128
BLK = 128
R = 3
G = 2
BLK_DEV = 4
NKEY = 3 + R + G
AXES = ("seq", "head")
LINE = 4
NQ = LINE * BLK_DEV
ROWS = NQ * BLK
NSHARD = 8
F32 = jnp.float32
BF16 = jnp.bfloat16


def moved(dev, ring, pair, line):
    h, s = dev % 4, dev // 4
    x, y, z = s // 8, (s // 4) % 2, s % 4
    if h % 2 == 0:
        x, z = (x + ring) % 4, (z + line) % 4
    else:
        z, x = (z + ring) % 4, (x + line) % 4
    y = (y + pair) % 2
    return ((x * 2 + y) * 4 + z) * 4 + h


def line_pos(dev):
    h, s = dev % 4, dev // 4
    return s % 4 if h % 2 == 0 else s // 8


DEVS = range(128)


def groups(step):
    seen, out = set(), []
    for d in DEVS:
        if d not in seen:
            out.append([d] + [step(d, k) for k in (1, 2, 3)])
            seen.update(out[-1])
    return out


LINES = groups(lambda d, k: moved(d, 0, 0, k))
RING = {k: [(d, moved(d, k, 0, 0)) for d in DEVS if line_pos(d) < 3] for k in (1, 2, 3)}
PAIR = [(d, moved(d, 0, 1, 0)) for d in DEVS if line_pos(d) < 3]
CORE = [(d, d ^ 1) for d in DEVS]
FAR = [(d, d ^ 2) for d in DEVS]


def send(x, perm):
    return lax.ppermute(x, AXES, perm)


def attend_kernel(table, qd_ref, *refs):
    kv_refs, gq_ref = refs[:NSHARD], refs[NSHARD]
    out_refs = refs[NSHARD + 1 : 2 * NSHARD + 1]
    kv, acc, kv_now, stage, in_sems, out_sems = refs[2 * NSHARD + 1 :]
    scale = HD ** (-0.5)
    loads = [
        pltpu.make_async_copy(kv_refs[m], kv.at[pl.ds(m * ROWS, ROWS)], in_sems.at[m])
        for m in range(NSHARD)
    ]
    for c in loads:
        c.start()

    def zero(n, carry):
        acc[pl.ds(pl.multiple_of(n * BLK, BLK), BLK), :] = jnp.zeros((BLK, 2 * HD), F32)
        return carry

    lax.fori_loop(0, NSHARD * NQ, zero, 0, unroll=2)
    for c in loads:
        c.wait()

    nt = (((1,), (1,)), ((), ()))
    nn = (((1,), (0,)), ((), ()))
    tn = (((0,), (0,)), ((), ()))

    def step(n, carry):
        rows = pl.ds(pl.multiple_of(n * BLK, BLK), BLK)
        q = qd_ref[rows, :HD]
        d = qd_ref[rows, HD:]
        at = [pl.multiple_of(table[n, j] * BLK, BLK) for j in range(NKEY)]
        for j in range(NKEY):
            kv_now[j * BLK : (j + 1) * BLK, :] = kv[pl.ds(at[j], BLK), :]
        scores = lax.dot_general(kv_now[:, :HD], q, nt, preferred_element_type=F32)
        slope = lax.dot_general(kv_now[:, HD:], d, nt, preferred_element_type=F32)
        peak = jnp.max(scores, axis=0, keepdims=True)
        e = jnp.exp((scores - peak) * scale)
        inv = 1.0 / jnp.sum(e, axis=0, keepdims=True)
        weighted = jnp.sum(e * slope, axis=0, keepdims=True) * inv
        probs = e * inv
        coeff = (probs * (slope - weighted)).astype(BF16)
        low = probs.astype(BF16)
        gq = lax.dot_general(coeff, kv_now[:, :HD], tn, preferred_element_type=F32)
        gq_ref[rows, :] = (gq * scale).astype(BF16)
        gk = lax.dot_general(coeff, q, nn, preferred_element_type=F32)
        gv = lax.dot_general(low, d, nn, preferred_element_type=F32)
        for j in range(NKEY):
            part = slice(j * BLK, (j + 1) * BLK)
            acc[pl.ds(at[j], BLK), :HD] += gk[part]
            acc[pl.ds(at[j], BLK), HD:] += gv[part]
        return carry

    lax.fori_loop(0, NQ, step, 0, unroll=2)

    stores = [pltpu.make_async_copy(stage.at[m], out_refs[m], out_sems.at[m]) for m in range(NSHARD)]
    for m in range(NSHARD):

        def put(n, carry, m=m):
            rows = pl.ds(pl.multiple_of(n * BLK, BLK), BLK)
            src = pl.ds(pl.multiple_of(m * ROWS + n * BLK, BLK), BLK)
            stage[m, rows, :HD] = (acc[src, :HD] * scale).astype(BF16)
            stage[m, rows, HD:] = acc[src, HD:].astype(BF16)
            return carry

        lax.fori_loop(0, NQ, put, 0, unroll=2)
        stores[m].start()
    for c in stores:
        c.wait()


def attend(table, qd, shards):
    shard = jax.ShapeDtypeStruct((ROWS, 2 * HD), BF16)
    vmem = pl.BlockSpec(memory_space=pltpu.VMEM)
    far = pl.BlockSpec(memory_space=pl.ANY)
    out = pl.pallas_call(
        attend_kernel,
        name="attend",
        out_shape=(jax.ShapeDtypeStruct((ROWS, HD), BF16),) + (shard,) * NSHARD,
        grid_spec=pltpu.PrefetchScalarGridSpec(
            num_scalar_prefetch=1,
            grid=(),
            in_specs=[vmem] + [far] * NSHARD,
            out_specs=(vmem,) + (far,) * NSHARD,
            scratch_shapes=[
                pltpu.VMEM((NSHARD * ROWS, 2 * HD), BF16),
                pltpu.VMEM((NSHARD * ROWS, 2 * HD), F32),
                pltpu.VMEM((NKEY * BLK, 2 * HD), BF16),
                pltpu.VMEM((NSHARD, ROWS, 2 * HD), BF16),
                pltpu.SemaphoreType.DMA((NSHARD,)),
                pltpu.SemaphoreType.DMA((NSHARD,)),
            ],
        ),
        compiler_params=pltpu.CompilerParams(vmem_limit_bytes=56 << 20),
    )(table, qd, *shards)
    return out[0], out[1:]


def add(*terms):
    return functools.reduce(lambda a, b: a + b, [t.astype(F32) for t in terms]).astype(BF16)


def exchange(x):
    return lax.all_to_all(x, AXES, 0, 0, axis_index_groups=LINES, tiled=True)


def deal(a, b):
    heads = [
        jnp.concatenate([a[:, p * HD : (p + 1) * HD], b[:, p * HD : (p + 1) * HD]], axis=1)
        for p in (0, 1, 2, 0)
    ]
    return exchange(jnp.concatenate(heads, axis=0))


def body(queries, keys, values, upstream_out, out_weight, qkv_weight, rand_links, global_links):
    s = lax.axis_index("seq")
    h = lax.axis_index("head")
    x, y, z = s // 8, (s // 4) % 2, s % 4
    core, far = h % 2, h // 2
    ring = jnp.where(core == 0, x, z)

    n = jnp.arange(NQ, dtype=jnp.int32)
    line = n // BLK_DEV
    seq = jnp.where(core == 0, (x * 2 + y) * 4 + line, (line * 2 + y) * 4 + z)
    block = seq * BLK_DEV + n % BLK_DEV
    total = rand_links.shape[0]
    mine = block[:, None, None] == jnp.arange(total, dtype=jnp.int32)[None, :, None]
    rand = jnp.sum(jnp.where(mine, rand_links[None], 0), axis=1)
    window = (block[:, None] + jnp.arange(-1, 2, dtype=jnp.int32)[None]) % total
    glob = jnp.broadcast_to(global_links[None], (NQ, G))
    key = jnp.concatenate([window, rand, glob], axis=1)
    ks = key // BLK_DEV
    kx, ky, kz = ks // 8, (ks // 4) % 2, ks % 4
    k_ring = jnp.where(core == 0, kx, kz)
    k_pos = jnp.where(core == 0, kz, kx)
    shard_of = jnp.where(ky == y, 0, 4) + (k_ring - ring) % 4
    table = (shard_of * LINE + k_pos) * BLK_DEV + key % BLK_DEV

    own = deal(keys, values)
    other = send(own, PAIR)
    next_, last = send(own, RING[3]), send(own, RING[1])
    across = send(own, RING[2])
    grad_ctx = lax.dot_general(
        upstream_out, out_weight, (((1,), (1,)), ((), ())), preferred_element_type=F32
    ).astype(BF16)
    grad_ctx, other = lax.optimization_barrier((grad_ctx, other))
    qd = deal(queries, grad_ctx)
    other_row = [other, send(other, RING[3]), send(across, PAIR), send(other, RING[1])]
    grad_q, parts = attend(table, qd, [own, next_, across, last] + other_row)

    corner = send(parts[6], PAIR)
    other_sum = add(parts[4], send(parts[5], RING[1]), send(parts[7], RING[3]))
    q_back = exchange(grad_q)
    sides = [send(parts[1], RING[1]), send(parts[3], RING[3])]
    other_sum = send(other_sum, PAIR)
    across = send(add(parts[2], corner), RING[2])
    kv_back = exchange(add(parts[0], *sides, across, other_sum))

    def tokens(back, lanes):
        back = back.reshape(LINE, BLK_DEV * BLK, -1)
        return jnp.concatenate([back[p, :, lanes] for p in range(3)], axis=1)

    grads = [
        tokens(q_back, slice(0, HD)),
        tokens(kv_back, slice(0, HD)),
        tokens(kv_back, slice(HD, 2 * HD)),
    ]
    weight = qkv_weight.reshape(3, 2, 2, qkv_weight.shape[1] // 4, qkv_weight.shape[2])

    def share(to_far, to_core):
        w = lax.dynamic_index_in_dim(weight, to_far, 1, keepdims=False)
        w = lax.dynamic_index_in_dim(w, to_core, 1, keepdims=False)
        return sum(
            lax.dot_general(w[j], g, (((1,), (1,)), ((), ())), preferred_element_type=F32)
            for j, g in enumerate(grads)
        ).astype(BF16)

    from_far = send(add(share(1 - far, core), send(share(1 - far, 1 - core), CORE)), FAR)
    here = send(share(far, 1 - core), CORE)
    return add(share(far, core), here, from_far)


def solution(mesh):
    in_specs = (
        P("seq", "head"),
        P("seq", "head"),
        P("seq", "head"),
        P("seq", None),
        P("head", None),
        P(None, None, "head"),
        P(),
        P(),
    )
    out_specs = P("head", "seq")
    return jax.shard_map(body, mesh=mesh, in_specs=in_specs, out_specs=out_specs, check_vma=False)
```

```python
import functools

import jax
import jax.numpy as jnp
from jax import lax
from jax.experimental import pallas as pl
from jax.experimental.pallas import tpu as pltpu
from jax.sharding import PartitionSpec as P

HD = 128
BLK = 128
R = 3
G = 2
BLK_DEV = 4
NKEY = 3 + R + G
AXES = ("seq", "head")
LINE = 4
NQ = LINE * BLK_DEV
ROWS = NQ * BLK
NSHARD = 8
F32 = jnp.float32
BF16 = jnp.bfloat16


def moved(dev, ring, pair, line):
    h, s = dev % 4, dev // 4
    x, y, z = s // 8, (s // 4) % 2, s % 4
    if h % 2 == 0:
        x, z = (x + ring) % 4, (z + line) % 4
    else:
        z, x = (z + ring) % 4, (x + line) % 4
    y = (y + pair) % 2
    return ((x * 2 + y) * 4 + z) * 4 + h


def line_pos(dev):
    h, s = dev % 4, dev // 4
    return s % 4 if h % 2 == 0 else s // 8


DEVS = range(128)


def groups(step):
    seen, out = set(), []
    for d in DEVS:
        if d not in seen:
            out.append([d] + [step(d, k) for k in (1, 2, 3)])
            seen.update(out[-1])
    return out


LINES = groups(lambda d, k: moved(d, 0, 0, k))
RING = {k: [(d, moved(d, k, 0, 0)) for d in DEVS if line_pos(d) < 3] for k in (1, 2, 3)}
PAIR = [(d, moved(d, 0, 1, 0)) for d in DEVS if line_pos(d) < 3]
SWAP = [(d, moved(d, 0, 1, 0)) for d in DEVS]
CORE = [(d, d ^ 1) for d in DEVS]
FAR = [(d, d ^ 2) for d in DEVS]


def send(x, perm):
    return lax.ppermute(x, AXES, perm)


def attend_kernel(table, qd_ref, *refs):
    kv_refs, gq_ref = refs[:NSHARD], refs[NSHARD]
    out_refs = refs[NSHARD + 1 : 2 * NSHARD + 1]
    kv, acc, kv_now, stage, in_sems, out_sems = refs[2 * NSHARD + 1 :]
    scale = HD ** (-0.5)
    loads = [
        pltpu.make_async_copy(kv_refs[m], kv.at[pl.ds(m * ROWS, ROWS)], in_sems.at[m])
        for m in range(NSHARD)
    ]
    for c in loads:
        c.start()

    def zero(n, carry):
        acc[pl.ds(pl.multiple_of(n * BLK, BLK), BLK), :] = jnp.zeros((BLK, 2 * HD), F32)
        return carry

    lax.fori_loop(0, NSHARD * NQ, zero, 0, unroll=2)
    for c in loads:
        c.wait()

    nt = (((1,), (1,)), ((), ()))
    nn = (((1,), (0,)), ((), ()))
    tn = (((0,), (0,)), ((), ()))

    def step(n, carry):
        rows = pl.ds(pl.multiple_of(n * BLK, BLK), BLK)
        q = qd_ref[rows, :HD]
        d = qd_ref[rows, HD:]
        at = [pl.multiple_of(table[n, j] * BLK, BLK) for j in range(NKEY)]
        for j in range(NKEY):
            kv_now[j * BLK : (j + 1) * BLK, :] = kv[pl.ds(at[j], BLK), :]
        scores = lax.dot_general(kv_now[:, :HD], q, nt, preferred_element_type=F32)
        slope = lax.dot_general(kv_now[:, HD:], d, nt, preferred_element_type=F32)
        peak = jnp.max(scores, axis=0, keepdims=True)
        e = jnp.exp((scores - peak) * scale)
        inv = 1.0 / jnp.sum(e, axis=0, keepdims=True)
        weighted = jnp.sum(e * slope, axis=0, keepdims=True) * inv
        probs = e * inv
        coeff = (probs * (slope - weighted)).astype(BF16)
        low = probs.astype(BF16)
        gq = lax.dot_general(coeff, kv_now[:, :HD], tn, preferred_element_type=F32)
        gq_ref[rows, :] = (gq * scale).astype(BF16)
        gk = lax.dot_general(coeff, q, nn, preferred_element_type=F32)
        gv = lax.dot_general(low, d, nn, preferred_element_type=F32)
        for j in range(NKEY):
            part = slice(j * BLK, (j + 1) * BLK)
            acc[pl.ds(at[j], BLK), :HD] += gk[part]
            acc[pl.ds(at[j], BLK), HD:] += gv[part]
        return carry

    lax.fori_loop(0, NQ, step, 0, unroll=2)

    stores = [pltpu.make_async_copy(stage.at[m], out_refs[m], out_sems.at[m]) for m in range(NSHARD)]
    for m in range(NSHARD):

        def put(n, carry, m=m):
            rows = pl.ds(pl.multiple_of(n * BLK, BLK), BLK)
            src = pl.ds(pl.multiple_of(m * ROWS + n * BLK, BLK), BLK)
            stage[m, rows, :HD] = (acc[src, :HD] * scale).astype(BF16)
            stage[m, rows, HD:] = acc[src, HD:].astype(BF16)
            return carry

        lax.fori_loop(0, NQ, put, 0, unroll=2)
        stores[m].start()
    for c in stores:
        c.wait()


def attend(table, qd, shards):
    shard = jax.ShapeDtypeStruct((ROWS, 2 * HD), BF16)
    vmem = pl.BlockSpec(memory_space=pltpu.VMEM)
    far = pl.BlockSpec(memory_space=pl.ANY)
    out = pl.pallas_call(
        attend_kernel,
        name="attend",
        out_shape=(jax.ShapeDtypeStruct((ROWS, HD), BF16),) + (shard,) * NSHARD,
        grid_spec=pltpu.PrefetchScalarGridSpec(
            num_scalar_prefetch=1,
            grid=(),
            in_specs=[vmem] + [far] * NSHARD,
            out_specs=(vmem,) + (far,) * NSHARD,
            scratch_shapes=[
                pltpu.VMEM((NSHARD * ROWS, 2 * HD), BF16),
                pltpu.VMEM((NSHARD * ROWS, 2 * HD), F32),
                pltpu.VMEM((NKEY * BLK, 2 * HD), BF16),
                pltpu.VMEM((NSHARD, ROWS, 2 * HD), BF16),
                pltpu.SemaphoreType.DMA((NSHARD,)),
                pltpu.SemaphoreType.DMA((NSHARD,)),
            ],
        ),
        compiler_params=pltpu.CompilerParams(vmem_limit_bytes=56 << 20),
    )(table, qd, *shards)
    return out[0], out[1:]


def after(x, other):
    return lax.optimization_barrier((x, other))[0]


def add(*terms):
    return functools.reduce(lambda a, b: a + b, [t.astype(F32) for t in terms]).astype(BF16)


def exchange(x):
    return lax.all_to_all(x, AXES, 0, 0, axis_index_groups=LINES, tiled=True)


def by_head(a, b):
    heads = [
        jnp.concatenate([a[:, p * HD : (p + 1) * HD], b[:, p * HD : (p + 1) * HD]], axis=1)
        for p in range(3)
    ]
    return jnp.concatenate(heads, axis=0)


def deal(heads):
    return exchange(jnp.concatenate([heads, heads[: BLK_DEV * BLK]], axis=0))


def body(queries, keys, values, upstream_out, out_weight, qkv_weight, rand_links, global_links):
    s = lax.axis_index("seq")
    h = lax.axis_index("head")
    x, y, z = s // 8, (s // 4) % 2, s % 4
    core, far = h % 2, h // 2
    ring = jnp.where(core == 0, x, z)

    n = jnp.arange(NQ, dtype=jnp.int32)
    line = n // BLK_DEV
    seq = jnp.where(core == 0, (x * 2 + y) * 4 + line, (line * 2 + y) * 4 + z)
    block = seq * BLK_DEV + n % BLK_DEV
    total = rand_links.shape[0]
    mine = block[:, None, None] == jnp.arange(total, dtype=jnp.int32)[None, :, None]
    rand = jnp.sum(jnp.where(mine, rand_links[None], 0), axis=1)
    window = (block[:, None] + jnp.arange(-1, 2, dtype=jnp.int32)[None]) % total
    glob = jnp.broadcast_to(global_links[None], (NQ, G))
    key = jnp.concatenate([window, rand, glob], axis=1)
    ks = key // BLK_DEV
    kx, ky, kz = ks // 8, (ks // 4) % 2, ks % 4
    k_ring = jnp.where(core == 0, kx, kz)
    k_pos = jnp.where(core == 0, kz, kx)
    shard_of = jnp.where(ky == y, 0, 4) + (k_ring - ring) % 4
    table = (shard_of * LINE + k_pos) * BLK_DEV + key % BLK_DEV

    heads = by_head(keys, values)
    swapped = send(heads, SWAP)
    own = deal(heads)
    across = send(own, RING[2])
    other = deal(swapped)
    next_, last = send(own, RING[3]), send(own, RING[1])
    corner = send(across, PAIR)
    grad_ctx = lax.dot_general(
        upstream_out, out_weight, (((1,), (1,)), ((), ())), preferred_element_type=F32
    ).astype(BF16)
    grad_ctx = after(grad_ctx, other)
    other_next, other_last = send(other, RING[3]), send(other, RING[1])
    qd = deal(by_head(queries, grad_ctx))
    grad_q, parts = attend(
        table, qd, [own, next_, across, last, other, other_next, corner, other_last]
    )

    corner = send(parts[6], PAIR)
    other_sum = add(parts[4], send(parts[5], RING[1]), send(parts[7], RING[3]))
    sides = [send(parts[1], RING[1]), send(parts[3], RING[3])]
    first = jnp.concatenate([other_sum, grad_q], axis=1)
    corner = after(corner, first)
    first = exchange(first).reshape(LINE, -1, 3 * HD)
    across = send(add(parts[2], corner), RING[2])
    for_pair = first[:3, :, : 2 * HD]
    across = after(across, for_pair)
    from_pair = send(for_pair, SWAP)
    second = exchange(add(parts[0], *sides, across)).reshape(LINE, -1, 2 * HD)
    kv_back = add(second[:3], from_pair)

    def tokens(back, lanes):
        return jnp.concatenate([back[p, :, lanes] for p in range(3)], axis=1)

    grads = [
        tokens(first, slice(2 * HD, 3 * HD)),
        tokens(kv_back, slice(0, HD)),
        tokens(kv_back, slice(HD, 2 * HD)),
    ]
    weight = qkv_weight.reshape(3, 2, 2, qkv_weight.shape[1] // 4, qkv_weight.shape[2])

    def share(to_far, to_core):
        w = lax.dynamic_index_in_dim(weight, to_far, 1, keepdims=False)
        w = lax.dynamic_index_in_dim(w, to_core, 1, keepdims=False)
        return sum(
            lax.dot_general(w[j], g, (((1,), (1,)), ((), ())), preferred_element_type=F32)
            for j, g in enumerate(grads)
        ).astype(BF16)

    from_far = send(add(share(1 - far, core), send(share(1 - far, 1 - core), CORE)), FAR)
    here = send(share(far, 1 - core), CORE)
    return add(share(far, core), here, from_far)


def solution(mesh):
    in_specs = (
        P("seq", "head"),
        P("seq", "head"),
        P("seq", "head"),
        P("seq", None),
        P("head", None),
        P(None, None, "head"),
        P(),
        P(),
    )
    out_specs = P("head", "seq")
    return jax.shard_map(body, mesh=mesh, in_specs=in_specs, out_specs=out_specs, check_vma=False)
```

```python
import functools

import jax
import jax.numpy as jnp
from jax import lax
from jax.experimental import pallas as pl
from jax.experimental.pallas import tpu as pltpu
from jax.sharding import PartitionSpec as P

HD = 128
BLK = 128
R = 3
G = 2
BLK_DEV = 4
NKEY = 3 + R + G
AXES = ("seq", "head")
LINE = 4
NQ = LINE * BLK_DEV
ROWS = NQ * BLK
NSHARD = 8
HALF = ROWS // 2
PIECES = [ROWS] * 6 + [HALF] * 2 + [ROWS]
STARTS = [sum(PIECES[:m]) for m in range(len(PIECES))]
NPIECE = len(PIECES)
F32 = jnp.float32
BF16 = jnp.bfloat16


def moved(dev, ring, pair, line):
    h, s = dev % 4, dev // 4
    x, y, z = s // 8, (s // 4) % 2, s % 4
    if h % 2 == 0:
        x, z = (x + ring) % 4, (z + line) % 4
    else:
        z, x = (z + ring) % 4, (x + line) % 4
    y = (y + pair) % 2
    return ((x * 2 + y) * 4 + z) * 4 + h


def line_pos(dev):
    h, s = dev % 4, dev // 4
    return s % 4 if h % 2 == 0 else s // 8


DEVS = range(128)


def groups(step):
    seen, out = set(), []
    for d in DEVS:
        if d not in seen:
            out.append([d] + [step(d, k) for k in (1, 2, 3)])
            seen.update(out[-1])
    return out


LINES = groups(lambda d, k: moved(d, 0, 0, k))
RING = {k: [(d, moved(d, k, 0, 0)) for d in DEVS if line_pos(d) < 3] for k in (1, 2, 3)}
PAIR = [(d, moved(d, 0, 1, 0)) for d in DEVS if line_pos(d) < 3]
CORE = [(d, d ^ 1) for d in DEVS]
FAR = [(d, d ^ 2) for d in DEVS]


def send(x, perm):
    return lax.ppermute(x, AXES, perm)


def attend_kernel(table, dealt_ref, *refs):
    kv_refs, gq_ref = refs[:NPIECE], refs[NPIECE]
    out_refs = refs[NPIECE + 1 : 2 * NPIECE + 1]
    qd_ref, kv, acc, kv_now, stage, in_sems, out_sems = refs[2 * NPIECE + 1 :]
    scale = HD ** (-0.5)
    loads = [
        pltpu.make_async_copy(kv_refs[m], kv.at[pl.ds(STARTS[m], PIECES[m])], in_sems.at[m])
        for m in range(NPIECE)
    ]
    side = BLK_DEV * BLK
    loads += [
        pltpu.make_async_copy(
            dealt_ref.at[m, 1], qd_ref.at[pl.ds(m * side, side)], in_sems.at[NPIECE + m]
        )
        for m in range(LINE)
    ]
    for c in loads:
        c.start()

    def zero(n, carry):
        acc[pl.ds(pl.multiple_of(n * BLK, BLK), BLK), :] = jnp.zeros((BLK, 2 * HD), F32)
        return carry

    lax.fori_loop(0, NSHARD * NQ, zero, 0, unroll=2)
    for c in loads:
        c.wait()

    nt = (((1,), (1,)), ((), ()))
    nn = (((1,), (0,)), ((), ()))
    tn = (((0,), (0,)), ((), ()))

    def step(n, carry):
        rows = pl.ds(pl.multiple_of(n * BLK, BLK), BLK)
        q = qd_ref[rows, :HD]
        d = qd_ref[rows, HD:]
        at = [pl.multiple_of(table[n, j] * BLK, BLK) for j in range(NKEY)]
        for j in range(NKEY):
            kv_now[j * BLK : (j + 1) * BLK, :] = kv[pl.ds(at[j], BLK), :]
        scores = lax.dot_general(kv_now[:, :HD], q, nt, preferred_element_type=F32)
        slope = lax.dot_general(kv_now[:, HD:], d, nt, preferred_element_type=F32)
        peak = jnp.max(scores, axis=0, keepdims=True)
        e = jnp.exp((scores - peak) * scale)
        inv = 1.0 / jnp.sum(e, axis=0, keepdims=True)
        weighted = jnp.sum(e * slope, axis=0, keepdims=True) * inv
        probs = e * inv
        coeff = (probs * (slope - weighted)).astype(BF16)
        low = probs.astype(BF16)
        gq = lax.dot_general(coeff, kv_now[:, :HD], tn, preferred_element_type=F32)
        gq_ref[rows, :] = (gq * scale).astype(BF16)
        gk = lax.dot_general(coeff, q, nn, preferred_element_type=F32)
        gv = lax.dot_general(low, d, nn, preferred_element_type=F32)
        for j in range(NKEY):
            part = slice(j * BLK, (j + 1) * BLK)
            acc[pl.ds(at[j], BLK), :HD] += gk[part]
            acc[pl.ds(at[j], BLK), HD:] += gv[part]
        return carry

    lax.fori_loop(0, NQ, step, 0, unroll=2)

    stores = [
        pltpu.make_async_copy(stage.at[pl.ds(STARTS[m], PIECES[m])], out_refs[m], out_sems.at[m])
        for m in range(NPIECE)
    ]
    for m in range(NPIECE):

        def put(n, carry, m=m):
            rows = pl.ds(pl.multiple_of(STARTS[m] + n * BLK, BLK), BLK)
            stage[rows, :HD] = (acc[rows, :HD] * scale).astype(BF16)
            stage[rows, HD:] = acc[rows, HD:].astype(BF16)
            return carry

        lax.fori_loop(0, PIECES[m] // BLK, put, 0, unroll=2)
        stores[m].start()
    for c in stores:
        c.wait()


def attend(table, dealt, shards):
    pieces = tuple(jax.ShapeDtypeStruct((rows, 2 * HD), BF16) for rows in PIECES)
    vmem = pl.BlockSpec(memory_space=pltpu.VMEM)
    far = pl.BlockSpec(memory_space=pltpu.HBM)
    out = pl.pallas_call(
        attend_kernel,
        name="attend",
        out_shape=(jax.ShapeDtypeStruct((ROWS, HD), BF16),) + pieces,
        grid_spec=pltpu.PrefetchScalarGridSpec(
            num_scalar_prefetch=1,
            grid=(),
            in_specs=[far] * (NPIECE + 1),
            out_specs=(vmem,) + (far,) * NPIECE,
            scratch_shapes=[
                pltpu.VMEM((ROWS, 2 * HD), BF16),
                pltpu.VMEM((NSHARD * ROWS, 2 * HD), BF16),
                pltpu.VMEM((NSHARD * ROWS, 2 * HD), F32),
                pltpu.VMEM((NKEY * BLK, 2 * HD), BF16),
                pltpu.VMEM((NSHARD * ROWS, 2 * HD), BF16),
                pltpu.SemaphoreType.DMA((NPIECE + LINE,)),
                pltpu.SemaphoreType.DMA((NPIECE,)),
            ],
        ),
        compiler_params=pltpu.CompilerParams(vmem_limit_bytes=56 << 20),
    )(table, dealt, *shards)
    return out[0], out[1:]


def after(x, other):
    return lax.optimization_barrier((x, other))[0]


def add(*terms):
    return functools.reduce(lambda a, b: a + b, [t.astype(F32) for t in terms]).astype(BF16)


def exchange(x):
    return lax.all_to_all(x, AXES, 0, 0, axis_index_groups=LINES, tiled=True)


def prepare_kernel(up_hbm, out_w_hbm, k_hbm, v_hbm, q_hbm, o_hbm, up, out_w, k, v, q, o, sems, out_sem):
    loads = [
        pltpu.make_async_copy(src, dst, sems.at[m])
        for m, (src, dst) in enumerate(
            ((out_w_hbm, out_w), (up_hbm, up), (k_hbm, k), (v_hbm, v), (q_hbm, q))
        )
    ]
    for c in loads:
        c.start()
    loads[0].wait()
    loads[1].wait()
    ctx = lax.dot_general(
        up[...], out_w[...], (((1,), (1,)), ((), ())), preferred_element_type=F32
    ).astype(BF16)
    for c in loads[2:]:
        c.wait()
    for slot, p in enumerate((0, 1, 2, 0)):
        lanes = slice(p * HD, (p + 1) * HD)
        o[slot, 0, :, :HD] = k[:, lanes]
        o[slot, 0, :, HD:] = v[:, lanes]
        o[slot, 1, :, :HD] = q[:, lanes]
        o[slot, 1, :, HD:] = ctx[:, lanes]
    store = pltpu.make_async_copy(o, o_hbm, out_sem)
    store.start()
    store.wait()


def prepare(upstream_out, out_weight, keys, values, queries):
    args = (upstream_out, out_weight, keys, values, queries)
    out = jax.ShapeDtypeStruct((LINE, 2, BLK_DEV * BLK, 2 * HD), BF16)
    far = pl.BlockSpec(memory_space=pltpu.HBM)
    return pl.pallas_call(
        prepare_kernel,
        name="prepare",
        out_shape=out,
        in_specs=[far] * len(args),
        out_specs=far,
        scratch_shapes=[pltpu.VMEM(a.shape, BF16) for a in args + (out,)]
        + [pltpu.SemaphoreType.DMA((len(args),)), pltpu.SemaphoreType.DMA],
        compiler_params=pltpu.CompilerParams(vmem_limit_bytes=58 << 20),
    )(*args)


def body(queries, keys, values, upstream_out, out_weight, qkv_weight, rand_links, global_links):
    s = lax.axis_index("seq")
    h = lax.axis_index("head")
    x, y, z = s // 8, (s // 4) % 2, s % 4
    core, far = h % 2, h // 2
    ring = jnp.where(core == 0, x, z)

    n = jnp.arange(NQ, dtype=jnp.int32)
    line = n // BLK_DEV
    seq = jnp.where(core == 0, (x * 2 + y) * 4 + line, (line * 2 + y) * 4 + z)
    block = seq * BLK_DEV + n % BLK_DEV
    total = rand_links.shape[0]
    mine = block[:, None, None] == jnp.arange(total, dtype=jnp.int32)[None, :, None]
    rand = jnp.sum(jnp.where(mine, rand_links[None], 0), axis=1)
    window = (block[:, None] + jnp.arange(-1, 2, dtype=jnp.int32)[None]) % total
    glob = jnp.broadcast_to(global_links[None], (NQ, G))
    key = jnp.concatenate([window, rand, glob], axis=1)
    ks = key // BLK_DEV
    kx, ky, kz = ks // 8, (ks // 4) % 2, ks % 4
    k_ring = jnp.where(core == 0, kx, kz)
    k_pos = jnp.where(core == 0, kz, kx)
    shard_of = jnp.where(ky == y, 0, 4) + (k_ring - ring) % 4
    table = (shard_of * LINE + k_pos) * BLK_DEV + key % BLK_DEV

    dealt = exchange(prepare(upstream_out, out_weight, keys, values, queries))
    own = dealt[:, 0].reshape(ROWS, 2 * HD)
    other = send(own, PAIR)
    next_, last = send(own, RING[3]), send(own, RING[1])
    across = send(own, RING[2])
    pieces = [own, next_, across, last, other, send(other, RING[3])]
    pieces += [send(across[:HALF], PAIR), send(other[HALF:], RING[2]), send(other, RING[1])]
    grad_q, parts = attend(table, dealt, pieces)

    corner = send(parts[6], PAIR)
    other_sum = [parts[4], send(parts[5], RING[1]), send(parts[8], RING[3])]
    corner_far = send(parts[7], RING[2])
    other_sum = jnp.concatenate(
        [add(*[t[:HALF] for t in other_sum]), add(*[t[HALF:] for t in other_sum], corner_far)]
    )
    corner = after(corner, other_sum)
    q_back = exchange(grad_q)
    sides = [send(parts[1], RING[1]), send(parts[3], RING[3])]
    other_sum = send(other_sum, PAIR)
    across = send(
        jnp.concatenate([add(parts[2][:HALF], corner), parts[2][HALF:]], axis=0), RING[2]
    )
    kv_back = exchange(add(parts[0], *sides, across, other_sum))

    def tokens(back, lanes):
        back = back.reshape(LINE, BLK_DEV * BLK, -1)
        return jnp.concatenate([back[p, :, lanes] for p in range(3)], axis=1)

    grads = [
        tokens(q_back, slice(0, HD)),
        tokens(kv_back, slice(0, HD)),
        tokens(kv_back, slice(HD, 2 * HD)),
    ]
    weight = qkv_weight.reshape(3, 2, 2, qkv_weight.shape[1] // 4, qkv_weight.shape[2])

    def share(to_far, to_core):
        w = lax.dynamic_index_in_dim(weight, to_far, 1, keepdims=False)
        w = lax.dynamic_index_in_dim(w, to_core, 1, keepdims=False)
        return sum(
            lax.dot_general(w[j], g, (((1,), (1,)), ((), ())), preferred_element_type=F32)
            for j, g in enumerate(grads)
        ).astype(BF16)

    from_far = send(add(share(1 - far, core), send(share(1 - far, 1 - core), CORE)), FAR)
    here = send(share(far, 1 - core), CORE)
    return add(share(far, core), here, from_far)


def solution(mesh):
    in_specs = (
        P("seq", "head"),
        P("seq", "head"),
        P("seq", "head"),
        P("seq", None),
        P("head", None),
        P(None, None, "head"),
        P(),
        P(),
    )
    out_specs = P("head", "seq")
    return jax.shard_map(body, mesh=mesh, in_specs=in_specs, out_specs=out_specs, check_vma=False)
```

```python
import functools

import jax
import jax.numpy as jnp
from jax import lax
from jax.experimental import pallas as pl
from jax.experimental.pallas import tpu as pltpu
from jax.sharding import PartitionSpec as P

HD = 128
BLK = 128
R = 3
G = 2
BLK_DEV = 4
NKEY = 3 + R + G
AXES = ("seq", "head")
LINE = 4
NQ = LINE * BLK_DEV
ROWS = NQ * BLK
NSHARD = 8
F32 = jnp.float32
BF16 = jnp.bfloat16


def moved(dev, ring, pair, line):
    h, s = dev % 4, dev // 4
    x, y, z = s // 8, (s // 4) % 2, s % 4
    if h % 2 == 0:
        x, z = (x + ring) % 4, (z + line) % 4
    else:
        z, x = (z + ring) % 4, (x + line) % 4
    y = (y + pair) % 2
    return ((x * 2 + y) * 4 + z) * 4 + h


def line_pos(dev):
    h, s = dev % 4, dev // 4
    return s % 4 if h % 2 == 0 else s // 8


DEVS = range(128)


def groups(step):
    seen, out = set(), []
    for d in DEVS:
        if d not in seen:
            out.append([d] + [step(d, k) for k in (1, 2, 3)])
            seen.update(out[-1])
    return out


LINES = groups(lambda d, k: moved(d, 0, 0, k))
RING = {k: [(d, moved(d, k, 0, 0)) for d in DEVS if line_pos(d) < 3] for k in (1, 2, 3)}
PAIR = [(d, moved(d, 0, 1, 0)) for d in DEVS if line_pos(d) < 3]
CORE = [(d, d ^ 1) for d in DEVS]
FAR = [(d, d ^ 2) for d in DEVS]


def send(x, perm):
    return lax.ppermute(x, AXES, perm)


def attend_kernel(table, qd_ref, *refs):
    kv_refs, gq_ref = refs[:NSHARD], refs[NSHARD]
    out_refs = refs[NSHARD + 1 : 2 * NSHARD + 1]
    kv, acc, kv_now, in_sems, out_sems = refs[2 * NSHARD + 1 :]
    scale = HD ** (-0.5)
    loads = [
        pltpu.make_async_copy(kv_refs[m], kv.at[pl.ds(m * ROWS, ROWS)], in_sems.at[m])
        for m in range(NSHARD)
    ]
    for c in loads:
        c.start()

    def zero(n, carry):
        acc[pl.ds(pl.multiple_of(n * BLK, BLK), BLK), :] = jnp.zeros((BLK, 2 * HD), F32)
        return carry

    lax.fori_loop(0, NSHARD * NQ, zero, 0, unroll=2)
    for c in loads:
        c.wait()

    nt = (((1,), (1,)), ((), ()))
    nn = (((1,), (0,)), ((), ()))
    tn = (((0,), (0,)), ((), ()))

    def step(n, carry):
        rows = pl.ds(pl.multiple_of(n * BLK, BLK), BLK)
        q = qd_ref[rows, :HD]
        d = qd_ref[rows, HD:]
        at = [pl.multiple_of(table[n, j] * BLK, BLK) for j in range(NKEY)]
        for j in range(NKEY):
            kv_now[j * BLK : (j + 1) * BLK, :] = kv[pl.ds(at[j], BLK), :]
        scores = lax.dot_general(kv_now[:, :HD], q, nt, preferred_element_type=F32)
        slope = lax.dot_general(kv_now[:, HD:], d, nt, preferred_element_type=F32)
        peak = jnp.max(scores, axis=0, keepdims=True)
        e = jnp.exp((scores - peak) * scale)
        inv = 1.0 / jnp.sum(e, axis=0, keepdims=True)
        weighted = jnp.sum(e * slope, axis=0, keepdims=True) * inv
        probs = e * inv
        coeff = (probs * (slope - weighted)).astype(BF16)
        low = probs.astype(BF16)
        gq = lax.dot_general(coeff, kv_now[:, :HD], tn, preferred_element_type=F32)
        gq_ref[rows, :] = (gq * scale).astype(BF16)
        gk = lax.dot_general(coeff, q, nn, preferred_element_type=F32)
        gv = lax.dot_general(low, d, nn, preferred_element_type=F32)
        for j in range(NKEY):
            part = slice(j * BLK, (j + 1) * BLK)
            acc[pl.ds(at[j], BLK), :HD] += gk[part]
            acc[pl.ds(at[j], BLK), HD:] += gv[part]
        return carry

    lax.fori_loop(0, NQ, step, 0, unroll=4)

    stores = [
        pltpu.make_async_copy(kv.at[pl.ds(m * ROWS, ROWS)], out_refs[m], out_sems.at[m])
        for m in range(NSHARD)
    ]
    for m in range(NSHARD):

        def put(n, carry, m=m):
            rows = pl.ds(pl.multiple_of(m * ROWS + n * BLK, BLK), BLK)
            kv[rows, :HD] = (acc[rows, :HD] * scale).astype(BF16)
            kv[rows, HD:] = acc[rows, HD:].astype(BF16)
            return carry

        lax.fori_loop(0, NQ, put, 0, unroll=2)
        stores[m].start()
    for c in stores:
        c.wait()


def attend(table, qd, shards):
    shard = jax.ShapeDtypeStruct((ROWS, 2 * HD), BF16)
    vmem = pl.BlockSpec(memory_space=pltpu.VMEM)
    far = pl.BlockSpec(memory_space=pl.ANY)
    out = pl.pallas_call(
        attend_kernel,
        name="attend",
        out_shape=(jax.ShapeDtypeStruct((ROWS, HD), BF16),) + (shard,) * NSHARD,
        grid_spec=pltpu.PrefetchScalarGridSpec(
            num_scalar_prefetch=1,
            grid=(),
            in_specs=[vmem] + [far] * NSHARD,
            out_specs=(vmem,) + (far,) * NSHARD,
            scratch_shapes=[
                pltpu.VMEM((NSHARD * ROWS, 2 * HD), BF16),
                pltpu.VMEM((NSHARD * ROWS, 2 * HD), F32),
                pltpu.VMEM((NKEY * BLK, 2 * HD), BF16),
                pltpu.SemaphoreType.DMA((NSHARD,)),
                pltpu.SemaphoreType.DMA((NSHARD,)),
            ],
        ),
        compiler_params=pltpu.CompilerParams(vmem_limit_bytes=32 << 20),
    )(table, qd, *shards)
    return out[0], out[1:]


def add(*terms):
    return functools.reduce(lambda a, b: a + b, [t.astype(F32) for t in terms]).astype(BF16)


def exchange(x):
    return lax.all_to_all(x, AXES, 0, 0, axis_index_groups=LINES, tiled=True)


def deal(a, b):
    heads = [
        jnp.concatenate([a[:, p * HD : (p + 1) * HD], b[:, p * HD : (p + 1) * HD]], axis=1)
        for p in (0, 1, 2, 0)
    ]
    return exchange(jnp.concatenate(heads, axis=0))


def body(queries, keys, values, upstream_out, out_weight, qkv_weight, rand_links, global_links):
    s = lax.axis_index("seq")
    h = lax.axis_index("head")
    x, y, z = s // 8, (s // 4) % 2, s % 4
    core, far = h % 2, h // 2
    ring = jnp.where(core == 0, x, z)

    n = jnp.arange(NQ, dtype=jnp.int32)
    line = n // BLK_DEV
    seq = jnp.where(core == 0, (x * 2 + y) * 4 + line, (line * 2 + y) * 4 + z)
    block = seq * BLK_DEV + n % BLK_DEV
    total = rand_links.shape[0]
    mine = block[:, None, None] == jnp.arange(total, dtype=jnp.int32)[None, :, None]
    rand = jnp.sum(jnp.where(mine, rand_links[None], 0), axis=1)
    window = (block[:, None] + jnp.arange(-1, 2, dtype=jnp.int32)[None]) % total
    glob = jnp.broadcast_to(global_links[None], (NQ, G))
    key = jnp.concatenate([window, rand, glob], axis=1)
    ks = key // BLK_DEV
    kx, ky, kz = ks // 8, (ks // 4) % 2, ks % 4
    k_ring = jnp.where(core == 0, kx, kz)
    k_pos = jnp.where(core == 0, kz, kx)
    shard_of = jnp.where(ky == y, 0, 4) + (k_ring - ring) % 4
    table = (shard_of * LINE + k_pos) * BLK_DEV + key % BLK_DEV

    own = deal(keys, values)
    other = send(own, PAIR)
    next_, last = send(own, RING[3]), send(own, RING[1])
    across = send(own, RING[2])
    grad_ctx = lax.dot_general(
        upstream_out, out_weight, (((1,), (1,)), ((), ())), preferred_element_type=F32
    ).astype(BF16)
    grad_ctx, other = lax.optimization_barrier((grad_ctx, other))
    qd = deal(queries, grad_ctx)
    other_row = [other, send(other, RING[3]), send(across, PAIR), send(other, RING[1])]
    grad_q, parts = attend(table, qd, [own, next_, across, last] + other_row)

    corner = send(parts[6], PAIR)
    other_sum = add(parts[4], send(parts[5], RING[1]), send(parts[7], RING[3]))
    q_back = exchange(grad_q)
    sides = [send(parts[1], RING[1]), send(parts[3], RING[3])]
    other_sum = send(other_sum, PAIR)
    across = send(add(parts[2], corner), RING[2])
    kv_back = exchange(add(parts[0], *sides, across, other_sum))

    def tokens(back, lanes):
        back = back.reshape(LINE, BLK_DEV * BLK, -1)
        return jnp.concatenate([back[p, :, lanes] for p in range(3)], axis=1)

    grads = [
        tokens(q_back, slice(0, HD)),
        tokens(kv_back, slice(0, HD)),
        tokens(kv_back, slice(HD, 2 * HD)),
    ]
    weight = qkv_weight.reshape(3, 2, 2, qkv_weight.shape[1] // 4, qkv_weight.shape[2])

    def share(to_far, to_core):
        w = lax.dynamic_index_in_dim(weight, to_far, 1, keepdims=False)
        w = lax.dynamic_index_in_dim(w, to_core, 1, keepdims=False)
        return sum(
            lax.dot_general(w[j], g, (((1,), (1,)), ((), ())), preferred_element_type=F32)
            for j, g in enumerate(grads)
        ).astype(BF16)

    from_far = send(add(share(1 - far, core), send(share(1 - far, 1 - core), CORE)), FAR)
    here = send(share(far, 1 - core), CORE)
    return add(share(far, core), here, from_far)


def solution(mesh):
    in_specs = (
        P("seq", "head"),
        P("seq", "head"),
        P("seq", "head"),
        P("seq", None),
        P("head", None),
        P(None, None, "head"),
        P(),
        P(),
    )
    out_specs = P("head", "seq")
    return jax.shard_map(body, mesh=mesh, in_specs=in_specs, out_specs=out_specs, check_vma=False)
```

```python
import functools

import jax
import jax.numpy as jnp
from jax import lax
from jax.experimental import pallas as pl
from jax.experimental.pallas import tpu as pltpu
from jax.sharding import PartitionSpec as P

HD = 128
BLK = 128
R = 3
G = 2
BLK_DEV = 4
NKEY = 3 + R + G
AXES = ("seq", "head")
LINE = 4
NQ = LINE * BLK_DEV
ROWS = NQ * BLK
NSHARD = 8
F32 = jnp.float32
BF16 = jnp.bfloat16


def moved(dev, ring, pair, line):
    h, s = dev % 4, dev // 4
    x, y, z = s // 8, (s // 4) % 2, s % 4
    if h % 2 == 0:
        x, z = (x + ring) % 4, (z + line) % 4
    else:
        z, x = (z + ring) % 4, (x + line) % 4
    y = (y + pair) % 2
    return ((x * 2 + y) * 4 + z) * 4 + h


def line_pos(dev):
    h, s = dev % 4, dev // 4
    return s % 4 if h % 2 == 0 else s // 8


DEVS = range(128)


def groups(step):
    seen, out = set(), []
    for d in DEVS:
        if d not in seen:
            out.append([d] + [step(d, k) for k in (1, 2, 3)])
            seen.update(out[-1])
    return out


LINES = groups(lambda d, k: moved(d, 0, 0, k))
RING = {k: [(d, moved(d, k, 0, 0)) for d in DEVS if line_pos(d) < 3] for k in (1, 2, 3)}
PAIR = [(d, moved(d, 0, 1, 0)) for d in DEVS if line_pos(d) < 3]
CORE = [(d, d ^ 1) for d in DEVS]
FAR = [(d, d ^ 2) for d in DEVS]


def send(x, perm):
    return lax.ppermute(x, AXES, perm)


def attend_kernel(table, qd_ref, *refs):
    kv_refs, gq_ref = refs[:NSHARD], refs[NSHARD]
    out_refs = refs[NSHARD + 1 : 2 * NSHARD + 1]
    kv, acc, kv_now, in_sems, out_sems = refs[2 * NSHARD + 1 :]
    scale = HD ** (-0.5)
    loads = [
        pltpu.make_async_copy(kv_refs[m], kv.at[pl.ds(m * ROWS, ROWS)], in_sems.at[m])
        for m in range(NSHARD)
    ]
    for c in loads:
        c.start()

    def zero(n, carry):
        acc[pl.ds(pl.multiple_of(n * BLK, BLK), BLK), :] = jnp.zeros((BLK, 2 * HD), F32)
        return carry

    lax.fori_loop(0, NSHARD * NQ, zero, 0, unroll=2)
    for c in loads:
        c.wait()

    nt = (((1,), (1,)), ((), ()))
    nn = (((1,), (0,)), ((), ()))
    tn = (((0,), (0,)), ((), ()))

    def step(n, carry):
        rows = pl.ds(pl.multiple_of(n * BLK, BLK), BLK)
        q = qd_ref[rows, :HD]
        d = qd_ref[rows, HD:]
        at = [pl.multiple_of(table[n, j] * BLK, BLK) for j in range(NKEY)]
        for j in range(NKEY):
            kv_now[j * BLK : (j + 1) * BLK, :] = kv[pl.ds(at[j], BLK), :]
        scores = lax.dot_general(kv_now[:, :HD], q, nt, preferred_element_type=F32)
        slope = lax.dot_general(kv_now[:, HD:], d, nt, preferred_element_type=F32)
        peak = jnp.max(scores, axis=0, keepdims=True)
        e = jnp.exp((scores - peak) * scale)
        inv = 1.0 / jnp.sum(e, axis=0, keepdims=True)
        weighted = jnp.sum(e * slope, axis=0, keepdims=True) * inv
        probs = e * inv
        coeff = (probs * (slope - weighted)).astype(BF16)
        low = probs.astype(BF16)
        gq = lax.dot_general(coeff, kv_now[:, :HD], tn, preferred_element_type=F32)
        gq_ref[rows, :] = (gq * scale).astype(BF16)
        gk = lax.dot_general(coeff, q, nn, preferred_element_type=F32)
        gv = lax.dot_general(low, d, nn, preferred_element_type=F32)
        for j in range(NKEY):
            part = slice(j * BLK, (j + 1) * BLK)
            acc[pl.ds(at[j], BLK), :HD] += gk[part]
            acc[pl.ds(at[j], BLK), HD:] += gv[part]
        return carry

    lax.fori_loop(0, NQ, step, 0, unroll=4)

    stores = [
        pltpu.make_async_copy(kv.at[pl.ds(m * ROWS, ROWS)], out_refs[m], out_sems.at[m])
        for m in range(NSHARD)
    ]
    for m in range(NSHARD):

        def put(n, carry, m=m):
            rows = pl.ds(pl.multiple_of(m * ROWS + n * BLK, BLK), BLK)
            kv[rows, :HD] = (acc[rows, :HD] * scale).astype(BF16)
            kv[rows, HD:] = acc[rows, HD:].astype(BF16)
            return carry

        lax.fori_loop(0, NQ, put, 0, unroll=2)
        stores[m].start()
    for c in stores:
        c.wait()


def attend(table, qd, shards):
    shard = jax.ShapeDtypeStruct((ROWS, 2 * HD), BF16)
    vmem = pl.BlockSpec(memory_space=pltpu.VMEM)
    far = pl.BlockSpec(memory_space=pl.ANY)
    out = pl.pallas_call(
        attend_kernel,
        name="attend",
        out_shape=(jax.ShapeDtypeStruct((ROWS, HD), BF16),) + (shard,) * NSHARD,
        grid_spec=pltpu.PrefetchScalarGridSpec(
            num_scalar_prefetch=1,
            grid=(),
            in_specs=[vmem] + [far] * NSHARD,
            out_specs=(vmem,) + (far,) * NSHARD,
            scratch_shapes=[
                pltpu.VMEM((NSHARD * ROWS, 2 * HD), BF16),
                pltpu.VMEM((NSHARD * ROWS, 2 * HD), F32),
                pltpu.VMEM((NKEY * BLK, 2 * HD), BF16),
                pltpu.SemaphoreType.DMA((NSHARD,)),
                pltpu.SemaphoreType.DMA((NSHARD,)),
            ],
        ),
        compiler_params=pltpu.CompilerParams(vmem_limit_bytes=32 << 20),
    )(table, qd, *shards)
    return out[0], out[1:]


def add(*terms):
    return functools.reduce(lambda a, b: a + b, [t.astype(F32) for t in terms]).astype(BF16)


def exchange(x):
    return lax.all_to_all(x, AXES, 0, 0, axis_index_groups=LINES, tiled=True)


def pack(a, b):
    heads = [
        jnp.concatenate([a[:, p * HD : (p + 1) * HD], b[:, p * HD : (p + 1) * HD]], axis=1)
        for p in (0, 1, 2, 0)
    ]
    return jnp.concatenate(heads, axis=0)


def prepare_kernel(up_hbm, out_w_hbm, q_hbm, o_hbm, up, out_w, q, o, sems, out_sem):
    loads = [
        pltpu.make_async_copy(src, dst, sems.at[m])
        for m, (src, dst) in enumerate(((out_w_hbm, out_w), (up_hbm, up), (q_hbm, q)))
    ]
    for c in loads:
        c.start()
    for c in loads:
        c.wait()
    ctx = lax.dot_general(
        up[...], out_w[...], (((1,), (1,)), ((), ())), preferred_element_type=F32
    ).astype(BF16)
    side = BLK_DEV * BLK
    for slot, p in enumerate((0, 1, 2, 0)):
        rows = slice(slot * side, (slot + 1) * side)
        lanes = slice(p * HD, (p + 1) * HD)
        o[rows, :HD] = q[:, lanes]
        o[rows, HD:] = ctx[:, lanes]
    store = pltpu.make_async_copy(o, o_hbm, out_sem)
    store.start()
    store.wait()


def prepare(upstream_out, out_weight, queries):
    args = (upstream_out, out_weight, queries)
    out = jax.ShapeDtypeStruct((ROWS, 2 * HD), BF16)
    far = pl.BlockSpec(memory_space=pl.ANY)
    return pl.pallas_call(
        prepare_kernel,
        name="prepare",
        out_shape=out,
        in_specs=[far] * len(args),
        out_specs=far,
        scratch_shapes=[pltpu.VMEM(a.shape, BF16) for a in args + (out,)]
        + [pltpu.SemaphoreType.DMA((len(args),)), pltpu.SemaphoreType.DMA],
        compiler_params=pltpu.CompilerParams(vmem_limit_bytes=58 << 20),
    )(*args)


def body(queries, keys, values, upstream_out, out_weight, qkv_weight, rand_links, global_links):
    s = lax.axis_index("seq")
    h = lax.axis_index("head")
    x, y, z = s // 8, (s // 4) % 2, s % 4
    core, far = h % 2, h // 2
    ring = jnp.where(core == 0, x, z)

    n = jnp.arange(NQ, dtype=jnp.int32)
    line = n // BLK_DEV
    seq = jnp.where(core == 0, (x * 2 + y) * 4 + line, (line * 2 + y) * 4 + z)
    block = seq * BLK_DEV + n % BLK_DEV
    total = rand_links.shape[0]
    mine = block[:, None, None] == jnp.arange(total, dtype=jnp.int32)[None, :, None]
    rand = jnp.sum(jnp.where(mine, rand_links[None], 0), axis=1)
    window = (block[:, None] + jnp.arange(-1, 2, dtype=jnp.int32)[None]) % total
    glob = jnp.broadcast_to(global_links[None], (NQ, G))
    key = jnp.concatenate([window, rand, glob], axis=1)
    ks = key // BLK_DEV
    kx, ky, kz = ks // 8, (ks // 4) % 2, ks % 4
    k_ring = jnp.where(core == 0, kx, kz)
    k_pos = jnp.where(core == 0, kz, kx)
    shard_of = jnp.where(ky == y, 0, 4) + (k_ring - ring) % 4
    table = (shard_of * LINE + k_pos) * BLK_DEV + key % BLK_DEV

    own = exchange(pack(keys, values))
    other = send(own, PAIR)
    next_, last = send(own, RING[3]), send(own, RING[1])
    across = send(own, RING[2])
    packed = prepare(upstream_out, out_weight, queries)
    corner = send(across, PAIR)
    other = lax.optimization_barrier((other, packed))[0]
    qd = exchange(packed)
    other_row = [other, send(other, RING[3]), corner, send(other, RING[1])]
    grad_q, parts = attend(table, qd, [own, next_, across, last] + other_row)

    corner = send(parts[6], PAIR)
    other_sum = add(parts[4], send(parts[5], RING[1]), send(parts[7], RING[3]))
    q_back = exchange(grad_q)
    sides = [send(parts[1], RING[1]), send(parts[3], RING[3])]
    other_sum = send(other_sum, PAIR)
    across = send(add(parts[2], corner), RING[2])
    kv_back = exchange(add(parts[0], *sides, across, other_sum))

    def tokens(back, lanes):
        back = back.reshape(LINE, BLK_DEV * BLK, -1)
        return jnp.concatenate([back[p, :, lanes] for p in range(3)], axis=1)

    grads = [
        tokens(q_back, slice(0, HD)),
        tokens(kv_back, slice(0, HD)),
        tokens(kv_back, slice(HD, 2 * HD)),
    ]
    weight = qkv_weight.reshape(3, 2, 2, qkv_weight.shape[1] // 4, qkv_weight.shape[2])

    def share(to_far, to_core):
        w = lax.dynamic_index_in_dim(weight, to_far, 1, keepdims=False)
        w = lax.dynamic_index_in_dim(w, to_core, 1, keepdims=False)
        return sum(
            lax.dot_general(w[j], g, (((1,), (1,)), ((), ())), preferred_element_type=F32)
            for j, g in enumerate(grads)
        ).astype(BF16)

    from_far = send(add(share(1 - far, core), send(share(1 - far, 1 - core), CORE)), FAR)
    here = send(share(far, 1 - core), CORE)
    return add(share(far, core), here, from_far)


def solution(mesh):
    in_specs = (
        P("seq", "head"),
        P("seq", "head"),
        P("seq", "head"),
        P("seq", None),
        P("head", None),
        P(None, None, "head"),
        P(),
        P(),
    )
    out_specs = P("head", "seq")
    return jax.shard_map(body, mesh=mesh, in_specs=in_specs, out_specs=out_specs, check_vma=False)
```

```python
import functools

import jax
import jax.numpy as jnp
from jax import lax
from jax.experimental import pallas as pl
from jax.experimental.pallas import tpu as pltpu
from jax.sharding import PartitionSpec as P

HD = 128
BLK = 128
R = 3
G = 2
BLK_DEV = 4
NKEY = 3 + R + G
AXES = ("seq", "head")
LINE = 4
NQ = LINE * BLK_DEV
ROWS = NQ * BLK
NSHARD = 8
F32 = jnp.float32
BF16 = jnp.bfloat16


def moved(dev, ring, pair, line):
    h, s = dev % 4, dev // 4
    x, y, z = s // 8, (s // 4) % 2, s % 4
    if h % 2 == 0:
        x, z = (x + ring) % 4, (z + line) % 4
    else:
        z, x = (z + ring) % 4, (x + line) % 4
    y = (y + pair) % 2
    return ((x * 2 + y) * 4 + z) * 4 + h


def line_pos(dev):
    h, s = dev % 4, dev // 4
    return s % 4 if h % 2 == 0 else s // 8


DEVS = range(128)


def groups(step):
    seen, out = set(), []
    for d in DEVS:
        if d not in seen:
            out.append([d] + [step(d, k) for k in (1, 2, 3)])
            seen.update(out[-1])
    return out


LINES = groups(lambda d, k: moved(d, 0, 0, k))
RING = {k: [(d, moved(d, k, 0, 0)) for d in DEVS if line_pos(d) < 3] for k in (1, 2, 3)}
PAIR = [(d, moved(d, 0, 1, 0)) for d in DEVS if line_pos(d) < 3]
CORE = [(d, d ^ 1) for d in DEVS]
FAR = [(d, d ^ 2) for d in DEVS]


def send(x, perm):
    return lax.ppermute(x, AXES, perm)


def attend_kernel(table, qd_ref, *refs):
    kv_refs, gq_ref = refs[:NSHARD], refs[NSHARD]
    out_refs = refs[NSHARD + 1 : 2 * NSHARD + 1]
    kv, acc, kv_now, in_sems, out_sems = refs[2 * NSHARD + 1 :]
    scale = HD ** (-0.5)
    loads = [
        pltpu.make_async_copy(kv_refs[m], kv.at[pl.ds(m * ROWS, ROWS)], in_sems.at[m])
        for m in range(NSHARD)
    ]
    for c in loads:
        c.start()

    def zero(n, carry):
        acc[pl.ds(pl.multiple_of(n * BLK, BLK), BLK), :] = jnp.zeros((BLK, 2 * HD), F32)
        return carry

    lax.fori_loop(0, NSHARD * NQ, zero, 0, unroll=2)
    for c in loads:
        c.wait()

    nt = (((1,), (1,)), ((), ()))
    nn = (((1,), (0,)), ((), ()))
    tn = (((0,), (0,)), ((), ()))

    def step(n, carry):
        rows = pl.ds(pl.multiple_of(n * BLK, BLK), BLK)
        q = qd_ref[rows, :HD]
        d = qd_ref[rows, HD:]
        at = [pl.multiple_of(table[n, j] * BLK, BLK) for j in range(NKEY)]
        for j in range(NKEY):
            kv_now[j * BLK : (j + 1) * BLK, :] = kv[pl.ds(at[j], BLK), :]
        scores = lax.dot_general(kv_now[:, :HD], q, nt, preferred_element_type=F32)
        slope = lax.dot_general(kv_now[:, HD:], d, nt, preferred_element_type=F32)
        peak = jnp.max(scores, axis=0, keepdims=True)
        e = jnp.exp((scores - peak) * scale)
        inv = 1.0 / jnp.sum(e, axis=0, keepdims=True)
        weighted = jnp.sum(e * slope, axis=0, keepdims=True) * inv
        probs = e * inv
        coeff = (probs * (slope - weighted)).astype(BF16)
        low = probs.astype(BF16)
        gq = lax.dot_general(kv_now[:, :HD], coeff, tn, preferred_element_type=F32).T
        gq_ref[rows, :] = (gq * scale).astype(BF16)
        gk = lax.dot_general(coeff, q, nn, preferred_element_type=F32)
        gv = lax.dot_general(low, d, nn, preferred_element_type=F32)
        for j in range(NKEY):
            part = slice(j * BLK, (j + 1) * BLK)
            acc[pl.ds(at[j], BLK), :HD] += gk[part]
            acc[pl.ds(at[j], BLK), HD:] += gv[part]
        return carry

    lax.fori_loop(0, NQ, step, 0, unroll=8)

    stores = [
        pltpu.make_async_copy(kv.at[pl.ds(m * ROWS, ROWS)], out_refs[m], out_sems.at[m])
        for m in range(NSHARD)
    ]
    for m in range(NSHARD):

        def put(n, carry, m=m):
            rows = pl.ds(pl.multiple_of(m * ROWS + n * BLK, BLK), BLK)
            kv[rows, :HD] = (acc[rows, :HD] * scale).astype(BF16)
            kv[rows, HD:] = acc[rows, HD:].astype(BF16)
            return carry

        lax.fori_loop(0, NQ, put, 0, unroll=2)
        stores[m].start()
    for c in stores:
        c.wait()


def attend(table, qd, shards):
    shard = jax.ShapeDtypeStruct((ROWS, 2 * HD), BF16)
    vmem = pl.BlockSpec(memory_space=pltpu.VMEM)
    far = pl.BlockSpec(memory_space=pl.ANY)
    out = pl.pallas_call(
        attend_kernel,
        name="attend",
        out_shape=(jax.ShapeDtypeStruct((ROWS, HD), BF16),) + (shard,) * NSHARD,
        grid_spec=pltpu.PrefetchScalarGridSpec(
            num_scalar_prefetch=1,
            grid=(),
            in_specs=[vmem] + [far] * NSHARD,
            out_specs=(vmem,) + (far,) * NSHARD,
            scratch_shapes=[
                pltpu.VMEM((NSHARD * ROWS, 2 * HD), BF16),
                pltpu.VMEM((NSHARD * ROWS, 2 * HD), F32),
                pltpu.VMEM((NKEY * BLK, 2 * HD), BF16),
                pltpu.SemaphoreType.DMA((NSHARD,)),
                pltpu.SemaphoreType.DMA((NSHARD,)),
            ],
        ),
        compiler_params=pltpu.CompilerParams(vmem_limit_bytes=32 << 20),
    )(table, qd, *shards)
    return out[0], out[1:]


def add(*terms):
    return functools.reduce(lambda a, b: a + b, [t.astype(F32) for t in terms]).astype(BF16)


def exchange(x):
    return lax.all_to_all(x, AXES, 0, 0, axis_index_groups=LINES, tiled=True)


def pack(a, b):
    heads = [
        jnp.concatenate([a[:, p * HD : (p + 1) * HD], b[:, p * HD : (p + 1) * HD]], axis=1)
        for p in (0, 1, 2, 0)
    ]
    return jnp.concatenate(heads, axis=0)


def prepare_kernel(up_hbm, out_w_hbm, q_hbm, o_hbm, up, out_w, q, o, sems, out_sem):
    loads = [
        pltpu.make_async_copy(src, dst, sems.at[m])
        for m, (src, dst) in enumerate(((out_w_hbm, out_w), (up_hbm, up), (q_hbm, q)))
    ]
    for c in loads:
        c.start()
    for c in loads:
        c.wait()
    ctx = lax.dot_general(
        up[...], out_w[...], (((1,), (1,)), ((), ())), preferred_element_type=F32
    ).astype(BF16)
    side = BLK_DEV * BLK
    for slot, p in enumerate((0, 1, 2, 0)):
        rows = slice(slot * side, (slot + 1) * side)
        lanes = slice(p * HD, (p + 1) * HD)
        o[rows, :HD] = q[:, lanes]
        o[rows, HD:] = ctx[:, lanes]
    store = pltpu.make_async_copy(o, o_hbm, out_sem)
    store.start()
    store.wait()


def prepare(upstream_out, out_weight, queries):
    args = (upstream_out, out_weight, queries)
    out = jax.ShapeDtypeStruct((ROWS, 2 * HD), BF16)
    far = pl.BlockSpec(memory_space=pl.ANY)
    return pl.pallas_call(
        prepare_kernel,
        name="prepare",
        out_shape=out,
        in_specs=[far] * len(args),
        out_specs=far,
        scratch_shapes=[pltpu.VMEM(a.shape, BF16) for a in args + (out,)]
        + [pltpu.SemaphoreType.DMA((len(args),)), pltpu.SemaphoreType.DMA],
        compiler_params=pltpu.CompilerParams(vmem_limit_bytes=58 << 20),
    )(*args)


def body(queries, keys, values, upstream_out, out_weight, qkv_weight, rand_links, global_links):
    s = lax.axis_index("seq")
    h = lax.axis_index("head")
    x, y, z = s // 8, (s // 4) % 2, s % 4
    core, far = h % 2, h // 2
    ring = jnp.where(core == 0, x, z)

    n = jnp.arange(NQ, dtype=jnp.int32)
    line = n // BLK_DEV
    seq = jnp.where(core == 0, (x * 2 + y) * 4 + line, (line * 2 + y) * 4 + z)
    block = seq * BLK_DEV + n % BLK_DEV
    total = rand_links.shape[0]
    mine = block[:, None, None] == jnp.arange(total, dtype=jnp.int32)[None, :, None]
    rand = jnp.sum(jnp.where(mine, rand_links[None], 0), axis=1)
    window = (block[:, None] + jnp.arange(-1, 2, dtype=jnp.int32)[None]) % total
    glob = jnp.broadcast_to(global_links[None], (NQ, G))
    key = jnp.concatenate([window, rand, glob], axis=1)
    ks = key // BLK_DEV
    kx, ky, kz = ks // 8, (ks // 4) % 2, ks % 4
    k_ring = jnp.where(core == 0, kx, kz)
    k_pos = jnp.where(core == 0, kz, kx)
    shard_of = jnp.where(ky == y, 0, 4) + (k_ring - ring) % 4
    table = (shard_of * LINE + k_pos) * BLK_DEV + key % BLK_DEV

    own = exchange(pack(keys, values))
    other = send(own, PAIR)
    next_, last = send(own, RING[3]), send(own, RING[1])
    across = send(own, RING[2])
    packed = prepare(upstream_out, out_weight, queries)
    corner = send(across, PAIR)
    other = lax.optimization_barrier((other, packed))[0]
    qd = exchange(packed)
    other_row = [other, send(other, RING[3]), corner, send(other, RING[1])]
    grad_q, parts = attend(table, qd, [own, next_, across, last] + other_row)

    corner = send(parts[6], PAIR)
    other_sum = add(parts[4], send(parts[5], RING[1]), send(parts[7], RING[3]))
    q_back = exchange(grad_q)
    sides = [send(parts[1], RING[1]), send(parts[3], RING[3])]
    other_sum = send(other_sum, PAIR)
    across = send(add(parts[2], corner), RING[2])
    kv_back = exchange(add(parts[0], *sides, across, other_sum))

    def tokens(back, lanes):
        back = back.reshape(LINE, BLK_DEV * BLK, -1)
        return jnp.concatenate([back[p, :, lanes] for p in range(3)], axis=1)

    grads = [
        tokens(q_back, slice(0, HD)),
        tokens(kv_back, slice(0, HD)),
        tokens(kv_back, slice(HD, 2 * HD)),
    ]
    weight = qkv_weight.reshape(3, 2, 2, qkv_weight.shape[1] // 4, qkv_weight.shape[2])

    def share(to_far, to_core):
        w = lax.dynamic_index_in_dim(weight, to_far, 1, keepdims=False)
        w = lax.dynamic_index_in_dim(w, to_core, 1, keepdims=False)
        return sum(
            lax.dot_general(w[j], g, (((1,), (1,)), ((), ())), preferred_element_type=F32)
            for j, g in enumerate(grads)
        ).astype(BF16)

    from_far = send(add(share(1 - far, core), send(share(1 - far, 1 - core), CORE)), FAR)
    here = send(share(far, 1 - core), CORE)
    return add(share(far, core), here, from_far)


def solution(mesh):
    in_specs = (
        P("seq", "head"),
        P("seq", "head"),
        P("seq", "head"),
        P("seq", None),
        P("head", None),
        P(None, None, "head"),
        P(),
        P(),
    )
    out_specs = P("head", "seq")
    return jax.shard_map(body, mesh=mesh, in_specs=in_specs, out_specs=out_specs, check_vma=False)
```
